256 devices in a mesh: seq: 16 (over z, x_hi), head: 16 (over x_lo, y, core).
Axes of the slice: x: 4 (x_hi: 2, x_lo: 2; x = x_hi * 2 + x_lo), y: 4, z: 8, core: 2. Of those that a mesh axis runs over, the one named last changes fastest.
Arguments:
- embedded: bfloat16 [2048, 8192], P('seq'), may hold values from -1457.645 to 1457.645
- norm_gain: bfloat16 [8192], replicated, may hold values from 0.5 to 1.5
- query_weight: bfloat16 [8192, 4096], P(None, 'head'), may hold values from -0.125 to 0.125
- query_bias: bfloat16 [4096], P('head'), may hold values from -15 to 15
- key_weight: bfloat16 [8192, 4, 128], P(None, None, 'head'), may hold values from -0.16572815 to 0.16572815
- value_weight: bfloat16 [8192, 4, 128], P(None, None, 'head'), may hold values from -0.0625 to 0.0625
- value_bias: bfloat16 [4, 128], P(None, 'head'), may hold values from -3 to 3
- image_rows: bfloat16 [768, 8192], P('seq'), may hold values from -6 to 6
- image_dest: int32 [768], P('seq'), may hold values from 0 to 2047, as said below
- doc_lengths: int32 [32], replicated, may hold values from 1 to 1152, 2048 in all
- block_mask: int32 [16, 16], P('seq'), may hold values from 0 to 1, as said below
Outputs:
- attention: bfloat16 [2048, 4096], P('seq', 'head')
The draws below stay inside these ranges and needn't reach their ends.
Inputs may be any that keep to these rules, and one draw needn't show every extreme that they name: `image_dest`: all positions differ. The 48 rows of one owner place at most 6 rows in any one shard of 128 positions, exactly 6 in some shard; one shard takes exactly 6 rows from every owner. `doc_lengths`: they add up to 2048; the longest is exactly 1152. `block_mask`: 1 on the diagonal, 0 above it.
All inputs are finite; a program needn't handle non-finite values.
Results may differ from the reference program's by a relative error of at most 0.011.
Values may be sent and summed in bfloat16 or wider, within the bound.
No kernel may reach another device: no remote copies, remote signals or barrier semaphores. Data moves between devices by JAX's collectives and lax.ppermute only.
A program may use at most 64 MiB of HBM per device.

```python
import math
import jax
import jax.numpy as jnp
import numpy as np
from jax import lax

D = 8192
HD = 128
GROUP = 8
BLK = 128
CAP = 6
TOK_DEV = 128
HEADS = 32
KVH = 4
SEQ = 2048
DOCS = 32
MOST_DOC = 1152
IMG_DEV = 48
IMG_ROWS = 768
N_SEQ = 16


def log_spread(key, length, lowest, highest):
    return jnp.exp(jax.random.uniform(key, (length,), jnp.float32, math.log(lowest), math.log(highest)))


def draw_embedded(key, part):
    column_scale = log_spread(jax.random.fold_in(key, 11), D, 0.5, 5.0)
    row_scale = log_spread(jax.random.fold_in(key, 12), SEQ, 0.5, 5.0)
    random_key = jax.random.fold_in(key, 13)
    random_part = jax.random.truncated_normal(random_key, -4.0, 4.0, (SEQ, D), jnp.float32)
    return (random_part * column_scale[None, :] * row_scale[:, None]).astype(jnp.bfloat16)


def draw_key_weight(key, part):
    deviation = 1.0 / math.sqrt(D)
    random_key = jax.random.fold_in(key, 21)
    return (jax.random.truncated_normal(random_key, -6.0, 6.0, (D, KVH, HD), jnp.float32) * deviation).astype(jnp.bfloat16)


def draw_query_bias(key, part):
    random_key = jax.random.fold_in(key, 31)
    return (0.5 * jax.random.truncated_normal(random_key, -3.0, 3.0, (HEADS * HD,), jnp.float32)).astype(jnp.bfloat16)


def draw_image_dest(key, part):
    shard_count = SEQ // TOK_DEV
    target_count = shard_count // 2 + 1
    anchor = jax.random.randint(jax.random.fold_in(key, 41), (), 0, shard_count)
    shuffle_keys = jax.random.split(jax.random.fold_in(key, 42), shard_count)
    shuffled = jax.vmap(lambda single: jax.random.permutation(single, shard_count - 1))(shuffle_keys) + 1
    offsets = jnp.concatenate([jnp.zeros((shard_count, 1), jnp.int32), shuffled.astype(jnp.int32)], axis=1)
    targets = ((anchor + offsets) % shard_count)[:, :target_count]
    shares = jax.random.randint(jax.random.fold_in(key, 43), (shard_count, 2), 0, CAP // 2 + 1).astype(jnp.int32)
    filled = jnp.full((shard_count, target_count - 3), CAP, jnp.int32)
    lengths = jnp.concatenate([filled, CAP - shares, jnp.sum(shares, axis=1, keepdims=True).astype(jnp.int32)], axis=1)
    bounds = jnp.cumsum(lengths, axis=1).astype(jnp.int32)
    row_index = jnp.arange(IMG_DEV)
    segment = jnp.sum((row_index[None, :, None] >= bounds[:, None, :]).astype(jnp.int32), axis=2)
    target = jnp.take_along_axis(targets, segment, axis=1).reshape(-1).astype(jnp.int32)
    one_hot = (target[:, None] == jnp.arange(shard_count)[None, :]).astype(jnp.int32)
    before = jnp.sum(one_hot * (jnp.cumsum(one_hot, axis=0) - one_hot), axis=1).astype(jnp.int32)
    place_keys = jax.random.split(jax.random.fold_in(key, 44), shard_count)
    places = jax.vmap(lambda single: jax.random.permutation(single, TOK_DEV))(place_keys).astype(jnp.int32)
    return (target * TOK_DEV + places[target, before]).astype(jnp.int32)


def draw_block_mask(key, part):
    blocks = SEQ // BLK
    coin_flips = jax.random.randint(jax.random.fold_in(key, 51), (blocks, blocks), 0, 2)
    block_index = jnp.arange(blocks)
    below = jnp.where(block_index[None, :] < block_index[:, None], coin_flips, 0)
    return jnp.where(block_index[:, None] == block_index[None, :], 1, below).astype(jnp.int32)


def steps_of(rng, extent, shards, least, high):
    def one(axis_at, parts):
        draws = jax.random.uniform(jax.random.fold_in(jax.random.fold_in(rng, 6), axis_at), (parts,), jnp.float32, least / len(shards), high / len(shards))
        return jnp.repeat(jnp.exp(draws), extent[axis_at] // parts).reshape((-1,) + (1,) * (len(extent) - axis_at - 1))

    level = one(*shards[0])
    for cut in shards[1:]:
        level = level * one(*cut)
    return level


def length_profile(amount, total, limit, skew):
    weights = [(1 << 20) // math.isqrt(grade ** skew) + 1 for grade in range(2, amount + 1)]
    spare, counts = total - limit - (amount - 1), [1] * (amount - 1)
    while spare > 0:
        movable = [i for i in range(amount - 1) if counts[i] < limit]
        pool, left = sum([weights[i] for i in movable]), spare
        for i in movable:
            more = min(limit - counts[i], max(1, left * weights[i] // pool), spare)
            counts[i] = counts[i] + more
            spare = spare - more
    return np.array([limit] + counts)


def uneven_parts(stream_key, amount, total, limit, slope):
    if amount == 2:
        one = jax.random.randint(stream_key, (), max(1, total - limit), min(limit, total - 1) + 1)
        return jnp.stack([one, total - one])
    sizes = jnp.asarray(length_profile(amount, total, limit, slope), jnp.int32)
    pairs = (amount - 1) // 2
    giver, receiver = sizes[1:1 + 2 * pairs:2], sizes[2:2 + 2 * pairs:2]
    margin = jnp.minimum(giver - 1, limit - receiver)
    shifted = jax.random.randint(jax.random.fold_in(stream_key, 1), (pairs,), 0, 1 << 20) % (margin + 1)
    sizes = sizes.at[1:1 + 2 * pairs:2].set(giver - shifted).at[2:2 + 2 * pairs:2].set(receiver + shifted)
    return sizes[jax.random.permutation(jax.random.fold_in(stream_key, 2), amount)]


def centred(stream_key, dims, scale, most, cuts=(), dtype=jnp.bfloat16):
    entries = jax.random.normal(stream_key, dims, jnp.float32) * scale
    if len(cuts) > 0:
        entries = steps_of(stream_key, dims, cuts, -0.22, 0.18) * entries
    return jnp.clip(entries, min=-most, max=most).astype(dtype)


def setup_inputs(seed: int = 0) -> dict:
    arg_keys = jax.random.split(jax.random.key(seed), 12)
    return {
        "embedded": draw_embedded(jax.random.fold_in(arg_keys[11], 71), 0),
        "norm_gain": jnp.clip(1.0 + 0.1 * jax.random.normal(arg_keys[1], (D,), jnp.float32), 0.5, 1.5).astype(jnp.bfloat16),
        "query_weight": centred(arg_keys[2], (D, HEADS * HD), (D // 4) ** -0.5, 0.125, ((1, 16),)),
        "query_bias": draw_query_bias(jax.random.fold_in(arg_keys[11], 71), 0),
        "key_weight": draw_key_weight(jax.random.fold_in(arg_keys[11], 71), 0),
        "value_weight": centred(arg_keys[5], (D, KVH, HD), D ** -0.5, 0.0625, ((2, 16),)),
        "value_bias": centred(arg_keys[6], (KVH, HD), 0.5, 3.0, ((1, 16),)),
        "image_rows": centred(arg_keys[7], (IMG_ROWS, D), 1.0, 6.0, ((0, 16),)),
        "image_dest": draw_image_dest(jax.random.fold_in(arg_keys[11], 71), 0),
        "doc_lengths": uneven_parts(arg_keys[9], DOCS, SEQ, MOST_DOC, 2).astype(jnp.int32),
        "block_mask": draw_block_mask(jax.random.fold_in(arg_keys[11], 71), 0),
    }


rope_base = 1000000.0
norm_eps = 1e-06

def held(array):
    return lax.optimization_barrier(array)

def doc_positions(token_index, doc_lengths):
    ends_at = jnp.cumsum(doc_lengths).astype(jnp.int32)
    starts = (ends_at - doc_lengths).astype(jnp.int32)
    doc_id = lax.optimization_barrier(jnp.sum((token_index[:, None] >= ends_at[None, :]).astype(jnp.int32), axis=1)).astype(jnp.int32)
    start_of = lax.optimization_barrier(jnp.max(jnp.where(token_index[:, None] >= starts[None, :], starts[None, :], 0), axis=1)).astype(jnp.int32)
    return (doc_id, (token_index - start_of).astype(jnp.int32))

def rope_tables(position, head_width):
    half_width = head_width // 2
    step_index = jnp.arange(half_width).astype(jnp.float32)
    inverse = jnp.power(jnp.float32(rope_base), -2.0 * step_index / head_width)
    angles = position.astype(jnp.float32)[:, None] * inverse[None, :]
    return (jnp.cos(angles), jnp.sin(angles))

def rotate(vectors, cosine_table, sine_table):
    half_width = vectors.shape[-1] // 2
    leading = vectors[..., :half_width]
    trailing = vectors[..., half_width:]
    cosine_part = cosine_table[:, None, :]
    sine_part = sine_table[:, None, :]
    return jnp.concatenate([leading * cosine_part - trailing * sine_part, trailing * cosine_part + leading * sine_part], axis=-1)

def reference(embedded, norm_gain, query_weight, query_bias, key_weight, value_weight, value_bias, image_rows, image_dest, doc_lengths, block_mask):
    merged = embedded.at[image_dest].set(image_rows)
    widened = merged.astype(jnp.float32)
    inverse_rms = lax.rsqrt(lax.optimization_barrier(jnp.mean(widened * widened, axis=1, keepdims=True)) + norm_eps)
    normed = held((widened * inverse_rms * norm_gain.astype(jnp.float32)[None, :]).astype(jnp.bfloat16))
    token_index = jnp.arange(SEQ).astype(jnp.int32)
    doc_id, position = doc_positions(token_index, doc_lengths)
    cosine_table, sine_table = rope_tables(position, HD)
    queries = jnp.dot(normed, query_weight, preferred_element_type=jnp.float32) + query_bias.astype(jnp.float32)[None, :]
    queries = held(rotate(queries.reshape(SEQ, HEADS, HD), cosine_table, sine_table).astype(jnp.bfloat16))
    key_raw = held(jnp.dot(normed, key_weight.reshape(D, KVH * HD), preferred_element_type=jnp.float32).astype(jnp.bfloat16))
    key_rot = held(rotate(key_raw.astype(jnp.float32).reshape(SEQ, KVH, HD), cosine_table, sine_table).astype(jnp.bfloat16))
    values = jnp.dot(normed, value_weight.reshape(D, KVH * HD), preferred_element_type=jnp.float32) + value_bias.reshape(KVH * HD).astype(jnp.float32)[None, :]
    values = held(values.astype(jnp.bfloat16)).reshape(SEQ, KVH, HD)
    key_wide = key_rot.astype(jnp.float32)
    value_wide = values.astype(jnp.float32)
    key_block = token_index // BLK
    scale_factor = 1.0 / math.sqrt(HD)

    def attend(block_number):
        row_start = (block_number * TOK_DEV).astype(jnp.int32)
        row_index = row_start + jnp.arange(TOK_DEV).astype(jnp.int32)
        block_queries = lax.dynamic_slice_in_dim(queries, row_start, TOK_DEV, 0).astype(jnp.float32)
        row_docs = lax.dynamic_slice_in_dim(doc_id, row_start, TOK_DEV, 0)
        mask_rows = lax.dynamic_slice_in_dim(block_mask, (block_number * (TOK_DEV // BLK)).astype(jnp.int32), TOK_DEV // BLK, 0)
        pair_open = mask_rows[jnp.arange(TOK_DEV) // BLK][:, key_block] == 1
        allowed = pair_open & (token_index[None, :] <= row_index[:, None]) & (doc_id[None, :] == row_docs[:, None])
        grouped = block_queries.reshape(TOK_DEV, KVH, GROUP, HD)
        scores = jnp.einsum('tkgd,skd->kgts', grouped, key_wide, precision=lax.Precision.HIGHEST) * scale_factor
        masked = jnp.where(allowed[None, None], scores, -jnp.inf)
        row_max = lax.optimization_barrier(jnp.max(masked, axis=3, keepdims=True))
        weights = jnp.where(allowed[None, None], jnp.exp(scores - row_max), 0.0)
        row_total = lax.optimization_barrier(jnp.sum(weights, axis=3))
        weights_low = held(weights.astype(jnp.bfloat16)).astype(jnp.float32)
        blended = jnp.einsum('kgts,skd->tkgd', weights_low, value_wide, precision=lax.Precision.HIGHEST)
        blended = blended / jnp.transpose(row_total, (2, 0, 1))[:, :, :, None]
        return blended.reshape(TOK_DEV, HEADS * HD).astype(jnp.bfloat16)
    blocks = lax.map(attend, jnp.arange(N_SEQ).astype(jnp.int32))
    return blocks.reshape(SEQ, HEADS * HD)
```

```python
import functools
import math

import jax
import jax.numpy as jnp
import numpy as np
from jax import lax
from jax.experimental import pallas as pl
from jax.experimental.pallas import tpu as pltpu
from jax.sharding import PartitionSpec as P

HD = 128
GROUP = 8
BLK = 128
CAP = 6
TOK = 128
IMG = 48
ROWS = TOK + IMG
TAIL = 16
PAY = ROWS + TAIL
N_SEQ = 16
N_HEAD = 16
DOCS = 32
KCH = 4
LIMIT = 60 << 20
SMALL = 12 << 20

rope_base = 1000000.0
norm_eps = 1e-06
BIG = 1.0e6
NEG = -1.0e30

f32 = jnp.float32
bf16 = jnp.bfloat16


def iota(shape, dim):
    return lax.broadcasted_iota(jnp.int32, shape, dim)


def fiota(shape, dim):
    return iota(shape, dim).astype(f32)


def dot_t(a, b):
    return lax.dot_general(a, b, (((1,), (1,)), ((), ())), preferred_element_type=f32)


def tdot(a, b):
    return lax.dot_general(a, b, (((0,), (0,)), ((), ())), preferred_element_type=f32)


def project_kernel(
    x_hbm, img_hbm, wq_hbm, wk_hbm, wv_hbm, gain_hbm, bq_hbm, bv_hbm, dest_hbm, invf_hbm, docs_ref,
    q_ref, kv_ref, tail_hbm, cs_hbm, start_hbm,
    xs, wqs, wkvs, gains, bqs, bvs, dests, invfs, tails, css, starts, sems, small_sems, out_sems,
):
    width = xs.shape[1]
    step = width // KCH
    copies = [
        pltpu.make_async_copy(x_hbm, xs.at[pl.ds(0, TOK)], sems.at[0]),
        pltpu.make_async_copy(img_hbm, xs.at[pl.ds(TOK, IMG)], sems.at[1]),
        pltpu.make_async_copy(wk_hbm, wkvs.at[pl.ds(0, 32)], sems.at[2]),
        pltpu.make_async_copy(wv_hbm, wkvs.at[pl.ds(32, 32)], sems.at[3]),
    ]
    for c in range(KCH):
        part = pl.ds(c * step, step)
        copies.append(pltpu.make_async_copy(wq_hbm.at[part], wqs.at[part], sems.at[4 + c]))
    small = [
        pltpu.make_async_copy(src, dst, small_sems.at[i])
        for i, (src, dst) in enumerate(
            ((dest_hbm, dests), (invf_hbm, invfs), (gain_hbm, gains), (bq_hbm, bqs), (bv_hbm, bvs))
        )
    ]
    for copy in small[:2] + copies[:2] + small[2:] + copies[2:]:
        copy.start()
    small[0].wait()
    small[1].wait()

    seq_place = lax.axis_index("seq")
    first = (seq_place * TOK).astype(f32)
    dest_row = dests[...].astype(f32)
    eye = iota((IMG, IMG), 0) == iota((IMG, IMG), 1)
    dest_col = jnp.sum(jnp.where(eye, dest_row, 0.0), axis=1, keepdims=True)
    hi_row = jnp.floor(dest_row * (1.0 / TOK))
    hi_col = jnp.floor(dest_col * (1.0 / TOK))
    lo_row = dest_row - TOK * hi_row
    lo_col = dest_col - TOK * hi_col

    index_col = jnp.concatenate([first + fiota((TOK, 1), 0), dest_col], axis=0)
    start_col = jnp.zeros((ROWS, 1), f32)
    begin = jnp.int32(0)
    for d in range(DOCS):
        begin_f = begin.astype(f32)
        start_col = jnp.where(index_col >= begin_f, begin_f, start_col)
        begin = begin + docs_ref[d]
    starts[...] = jnp.broadcast_to(start_col[:TOK], (TOK, HD))
    angles = (index_col - start_col) * invfs[...]
    cosine = jnp.cos(angles)
    sine = jnp.sin(angles)
    css[0] = cosine
    css[1] = jnp.where(iota((ROWS, HD), 1) < HD // 2, -sine, sine)

    earlier = iota((IMG, IMG), 0) < iota((IMG, IMG), 1)
    later = iota((IMG, IMG), 0) > iota((IMG, IMG), 1)
    same = hi_col == hi_row
    rank_row = jnp.sum(jnp.where(same & earlier, 1.0, 0.0), axis=0, keepdims=True)
    rank_col = jnp.sum(jnp.where(same & later, 1.0, 0.0), axis=1, keepdims=True)
    count = N_SEQ * TAIL
    line = iota((count, IMG), 0)
    here = hi_row == (line // TAIL).astype(f32)
    slot = (line % TAIL).astype(f32)
    offsets = jnp.where(here & (slot == 14.0), lo_row + 1.0, 0.0).astype(bf16)
    lane = iota((IMG, HD), 1)
    ranked = jnp.where((rank_col == lane.astype(f32)) & (lane < CAP), 1.0, 0.0).astype(bf16)
    tail = jnp.dot(offsets, ranked, preferred_element_type=f32)
    spread = (lane % 64) == iota((IMG, HD), 0)
    unused = (iota((1, HD), 1) % 64) >= IMG
    hi_two = jnp.where(unused, 99.0, jnp.sum(jnp.where(spread, hi_col, 0.0), axis=0, keepdims=True))
    lo_two = jnp.sum(jnp.where(spread, lo_col, 0.0), axis=0, keepdims=True)
    wide_slot = iota((count, HD), 0) % TAIL
    tail = tail + jnp.where(wide_slot == 12, hi_two, jnp.where(wide_slot == 13, lo_two, 0.0))

    outs = [
        pltpu.make_async_copy(css, cs_hbm, out_sems.at[0]),
        pltpu.make_async_copy(starts, start_hbm, out_sems.at[1]),
        pltpu.make_async_copy(tails, tail_hbm, out_sems.at[2]),
    ]
    outs[0].start()
    outs[1].start()

    inverse = []
    for i, rows in enumerate((pl.ds(0, TOK), pl.ds(TOK, IMG))):
        copies[i].wait()
        squares = jnp.zeros((rows.size, HD), f32)
        for c in range(width // HD):
            wide = xs[rows, c * HD : (c + 1) * HD].astype(f32)
            squares = squares + wide * wide
        inverse.append(
            lax.rsqrt(jnp.sum(squares, axis=1, keepdims=True) * (1.0 / width) + norm_eps)
        )
    inverse = jnp.concatenate(inverse, axis=0)

    for copy in small[2:] + copies[2:4]:
        copy.wait()
    queries = jnp.broadcast_to(bqs[...].astype(f32).reshape(1, 2 * HD), (ROWS, 2 * HD))
    kv = jnp.zeros((ROWS, 64), f32)
    for c in range(KCH):
        copies[4 + c].wait()
        part = pl.ds(c * step, step)
        gain = gains[part].astype(f32).reshape(1, step)
        normed = (xs[:, part].astype(f32) * inverse * gain).astype(bf16)
        kv = kv + dot_t(normed, wkvs[:, part])
        queries = queries + jnp.dot(normed, wqs[part, :], preferred_element_type=f32)

    kv = jnp.concatenate([kv, jnp.zeros((ROWS, 64), f32)], axis=1)
    kv = jnp.concatenate([kv, jnp.zeros((256 - ROWS, 128), f32)], axis=0)
    kv_t = jnp.transpose(kv)
    eye8 = iota((8, 8), 0) == iota((8, 8), 1)
    for g in range(4):
        key = kv_t[8 * g : 8 * g + 8].astype(bf16)
        bias_row = bvs[g : g + 1, :].astype(f32)
        bias = jnp.sum(jnp.where(eye8, bias_row, 0.0), axis=1, keepdims=True)
        value = (kv_t[32 + 8 * g : 40 + 8 * g] + bias).astype(bf16)
        for j in range(2):
            kv_ref[4 * g + 2 * j] = key
            kv_ref[4 * g + 2 * j + 1] = value

    cosine = css[0]
    sine = css[1]
    for e in range(2):
        v = queries[:, e * HD : (e + 1) * HD]
        v = (v * cosine + pltpu.roll(v, HD // 2, 1) * sine).astype(bf16)
        q_ref[e] = v[:TOK]
        pick = here & (rank_row == slot - CAP * e) & (slot >= CAP * e) & (slot < CAP * e + CAP)
        tail = tail + jnp.dot(
            jnp.where(pick, 1.0, 0.0).astype(bf16), v[TOK:], preferred_element_type=f32
        )
    tails[...] = tail.astype(bf16).reshape(N_SEQ, TAIL, HD)
    outs[2].start()
    for out in outs:
        out.wait()


def panel_kernel(kv_ref, cs_ref, tail_ref, pay_ref):
    is_key = lax.axis_index("head") % 2 == 0
    panel = jnp.transpose(kv_ref[...].astype(f32).reshape(HD, 256))[:ROWS]
    cosine = jnp.where(is_key, cs_ref[0], 1.0)
    sine = jnp.where(is_key, cs_ref[1], 0.0)
    panel = (panel * cosine + pltpu.roll(panel, HD // 2, 1) * sine).astype(bf16)
    for p in range(N_SEQ):
        pay_ref[p, 0:ROWS, :] = panel
        pay_ref[p, ROWS:PAY, :] = tail_ref[p]


def place_kernel(q_ref, mine_ref, mask_ref, merged_ref, where_ref):
    tails = mine_ref[:, ROWS:PAY, :].astype(f32)
    hi_all = tails[:, 12, :]
    lo_all = tails[:, 13, :]
    slots = tails[:, 14, :]
    count = N_SEQ * TAIL
    owner = iota((count, N_SEQ), 0) // TAIL == iota((count, N_SEQ), 1)
    spread = jnp.dot(
        jnp.where(owner, 1.0, 0.0).astype(bf16), slots.astype(bf16), preferred_element_type=f32
    )
    line = iota((count, HD), 0) % TAIL
    lane = iota((count, HD), 1)
    flat = mine_ref[:, ROWS:PAY, :].reshape(count, HD)
    for e in range(2):
        slot = line - CAP * e
        used = (slot >= 0) & (slot < CAP)
        offset = jnp.sum(jnp.where(used & (lane == slot), spread, 0.0), axis=1, keepdims=True)
        place = jnp.where(offset == lane.astype(f32) + 1.0, 1.0, 0.0).astype(bf16)
        moved = tdot(place, flat)
        taken = tdot(place, jnp.ones((count, HD), bf16))
        merged_ref[e * TOK : (e + 1) * TOK, :] = jnp.where(taken > 0.5, moved.astype(bf16), q_ref[e])

    low_half = iota((1, HD), 1) < 64
    covered = jnp.zeros((N_SEQ, HD), f32)
    for m in range(N_SEQ // 2):
        hi = jnp.where(low_half, hi_all[2 * m : 2 * m + 1], hi_all[2 * m + 1 : 2 * m + 2])
        lo = jnp.where(low_half, lo_all[2 * m : 2 * m + 1], lo_all[2 * m + 1 : 2 * m + 2])
        hi_hot = jnp.where(hi == fiota((N_SEQ, HD), 0), 1.0, 0.0).astype(bf16)
        lo_hot = jnp.where(lo == fiota((HD, HD), 0), 1.0, 0.0).astype(bf16)
        covered = covered + dot_t(hi_hot, lo_hot)
        seen = jnp.zeros((1, HD), f32)
        for b in range(N_SEQ):
            seen = jnp.where(hi == float(b), mask_ref[0, b].astype(f32), seen)
        where_ref[N_SEQ + m : N_SEQ + m + 1, :] = jnp.where(seen > 0.5, hi * float(TOK) + lo, BIG)
    for b in range(N_SEQ):
        free = (covered[b : b + 1] < 0.5) & (mask_ref[0, b] == 1)
        where_ref[b : b + 1, :] = jnp.where(free, float(TOK * b) + fiota((1, HD), 1), BIG)


def attend_kernel(q_ref, where_ref, start_ref, mine_ref, other_ref, out_ref, scores):
    is_key = lax.axis_index("head") % 2 == 0
    first = (lax.axis_index("seq") * TOK).astype(f32)
    tiles = N_SEQ + N_SEQ // 2
    slope = math.log2(math.e) / math.sqrt(HD)

    def tile_of(ref, t):
        if t < N_SEQ:
            return ref[t, 0:TOK, :]
        m = t - N_SEQ
        return ref[2 * m : 2 * m + 2, TOK:PAY, :].reshape(HD, HD)

    def attend(keys, values):
        queries = q_ref[...]
        position = first + fiota((TOK, HD), 0)
        start = start_ref[...]
        top = jnp.full((2 * TOK, HD), NEG, f32)
        for t in range(tiles):
            where = where_ref[t : t + 1, :]
            allowed = (where <= position) & (where >= start)
            allowed = jnp.concatenate([allowed, allowed], axis=0)
            score = jnp.where(allowed, dot_t(queries, tile_of(keys, t)), NEG)
            scores[t] = score
            top = jnp.maximum(top, score)
        top = jnp.max(top, axis=1, keepdims=True)
        total = jnp.zeros((2 * TOK, HD), f32)
        mix = jnp.zeros((2 * TOK, HD), f32)
        for t in range(tiles):
            weight = jnp.exp2((scores[t] - top) * slope)
            total = total + weight
            mix = mix + jnp.dot(weight.astype(bf16), tile_of(values, t), preferred_element_type=f32)
        mix = mix / jnp.sum(total, axis=1, keepdims=True)
        out_ref[:, 0:HD] = mix[:TOK].astype(bf16)
        out_ref[:, HD : 2 * HD] = mix[TOK:].astype(bf16)

    @pl.when(is_key)
    def _():
        attend(mine_ref, other_ref)

    @pl.when(jnp.logical_not(is_key))
    def _():
        attend(other_ref, mine_ref)


def vmem():
    return pl.BlockSpec(memory_space=pltpu.VMEM)


def body(
    embedded,
    norm_gain,
    query_weight,
    query_bias,
    key_weight,
    value_weight,
    value_bias,
    image_rows,
    image_dest,
    doc_lengths,
    block_mask,
):
    width = embedded.shape[1]
    half = np.arange(HD) % (HD // 2)
    inverse = jnp.asarray((rope_base ** (-2.0 * half / HD)).astype(np.float32)[None, :])
    hbm = pl.BlockSpec(memory_space=pltpu.HBM)
    smem = pl.BlockSpec(memory_space=pltpu.SMEM)
    key_t = jnp.transpose(key_weight, (1, 2, 0)).reshape(32, width)
    value_t = jnp.transpose(value_weight, (1, 2, 0)).reshape(32, width)
    queries, kv_send, tail, tables, start = pl.pallas_call(
        project_kernel,
        name="project",
        out_shape=(
            jax.ShapeDtypeStruct((2, TOK, HD), bf16),
            jax.ShapeDtypeStruct((N_HEAD, 8, 256), bf16),
            jax.ShapeDtypeStruct((N_SEQ, TAIL, HD), bf16),
            jax.ShapeDtypeStruct((2, ROWS, HD), f32),
            jax.ShapeDtypeStruct((TOK, HD), f32),
        ),
        in_specs=[hbm] * 10 + [smem],
        out_specs=(vmem(), vmem(), hbm, hbm, hbm),
        scratch_shapes=[
            pltpu.VMEM((ROWS, width), bf16),
            pltpu.VMEM((width, 2 * HD), bf16),
            pltpu.VMEM((64, width), bf16),
            pltpu.VMEM((width,), bf16),
            pltpu.VMEM((2 * HD,), bf16),
            pltpu.VMEM((4, 8), bf16),
            pltpu.VMEM((1, IMG), jnp.int32),
            pltpu.VMEM((1, HD), f32),
            pltpu.VMEM((N_SEQ, TAIL, HD), bf16),
            pltpu.VMEM((2, ROWS, HD), f32),
            pltpu.VMEM((TOK, HD), f32),
            pltpu.SemaphoreType.DMA((4 + KCH,)),
            pltpu.SemaphoreType.DMA((5,)),
            pltpu.SemaphoreType.DMA((3,)),
        ],
        compiler_params=pltpu.CompilerParams(vmem_limit_bytes=LIMIT),
    )(
        embedded, image_rows, query_weight, key_t, value_t, norm_gain, query_bias,
        value_bias, image_dest[None, :], inverse, doc_lengths,
    )
    kv_mine = lax.all_to_all(kv_send, "head", 0, 0)
    payload = pl.pallas_call(
        panel_kernel,
        name="panel",
        out_shape=jax.ShapeDtypeStruct((N_SEQ, PAY, HD), bf16),
        in_specs=[vmem()] * 3,
        out_specs=vmem(),
        compiler_params=pltpu.CompilerParams(vmem_limit_bytes=LIMIT),
    )(kv_mine, tables, tail)
    mine = lax.all_to_all(payload, "seq", 0, 0)
    other = lax.ppermute(mine, "head", [(i, i ^ 1) for i in range(N_HEAD)])
    merged, where = pl.pallas_call(
        place_kernel,
        name="place",
        out_shape=(
            jax.ShapeDtypeStruct((2 * TOK, HD), bf16),
            jax.ShapeDtypeStruct((N_SEQ + N_SEQ // 2, HD), f32),
        ),
        in_specs=[vmem(), vmem(), smem],
        out_specs=(vmem(), vmem()),
        compiler_params=pltpu.CompilerParams(vmem_limit_bytes=SMALL),
        cost_estimate=pl.CostEstimate(flops=1 << 28, bytes_accessed=1 << 20, transcendentals=0),
    )(queries, mine, block_mask)
    return pl.pallas_call(
        attend_kernel,
        name="attend",
        out_shape=jax.ShapeDtypeStruct((TOK, 2 * HD), bf16),
        in_specs=[vmem()] * 5,
        out_specs=vmem(),
        scratch_shapes=[pltpu.VMEM((N_SEQ + N_SEQ // 2, 2 * TOK, HD), f32)],
        compiler_params=pltpu.CompilerParams(vmem_limit_bytes=SMALL),
    )(merged, where, start, mine, other)


def solution(mesh):
    in_specs = (
        P("seq", None),
        P(),
        P(None, "head"),
        P("head"),
        P(None, None, "head"),
        P(None, None, "head"),
        P(None, "head"),
        P("seq", None),
        P("seq"),
        P(),
        P("seq", None),
    )
    out_specs = P("seq", "head")
    return jax.shard_map(body, mesh=mesh, in_specs=in_specs, out_specs=out_specs, check_vma=False)
```

```python
import functools
import math

import jax
import jax.numpy as jnp
import numpy as np
from jax import lax
from jax.experimental import pallas as pl
from jax.experimental.pallas import tpu as pltpu
from jax.sharding import PartitionSpec as P

HD = 128
GROUP = 8
BLK = 128
CAP = 6
TOK = 128
IMG = 48
ROWS = TOK + IMG
TAIL = 16
PAY = ROWS + TAIL
N_SEQ = 16
N_HEAD = 16
DOCS = 32
KCH = 4
LIMIT = 60 << 20
SMALL = 12 << 20

rope_base = 1000000.0
norm_eps = 1e-06
BIG = 1.0e6
NEG = -1.0e30

f32 = jnp.float32
bf16 = jnp.bfloat16


def iota(shape, dim):
    return lax.broadcasted_iota(jnp.int32, shape, dim)


def fiota(shape, dim):
    return iota(shape, dim).astype(f32)


def dot_t(a, b):
    return lax.dot_general(a, b, (((1,), (1,)), ((), ())), preferred_element_type=f32)


def tdot(a, b):
    return lax.dot_general(a, b, (((0,), (0,)), ((), ())), preferred_element_type=f32)


def project_kernel(
    x_hbm, img_hbm, wq_hbm, wk_hbm, wv_hbm, gain_hbm, bq_hbm, bv_hbm, dest_hbm, invf_hbm, docs_ref,
    q_hbm, kv_hbm, tail_hbm, cs_hbm, start_hbm,
    q_ref, kv_ref, xs, wqs, wkvs, gains, bqs, bvs, dests, invfs, tails, css, starts, sems, small_sems, out_sems,
):
    width = xs.shape[1]
    step = width // KCH
    copies = [
        pltpu.make_async_copy(x_hbm, xs.at[pl.ds(0, TOK)], sems.at[0]),
        pltpu.make_async_copy(img_hbm, xs.at[pl.ds(TOK, IMG)], sems.at[1]),
        pltpu.make_async_copy(wk_hbm, wkvs.at[pl.ds(0, 32)], sems.at[2]),
        pltpu.make_async_copy(wv_hbm, wkvs.at[pl.ds(32, 32)], sems.at[3]),
    ]
    for c in range(KCH):
        part = pl.ds(c * step, step)
        copies.append(pltpu.make_async_copy(wq_hbm.at[part], wqs.at[part], sems.at[4 + c]))
    small = [
        pltpu.make_async_copy(src, dst, small_sems.at[i])
        for i, (src, dst) in enumerate(
            ((dest_hbm, dests), (invf_hbm, invfs), (gain_hbm, gains), (bq_hbm, bqs), (bv_hbm, bvs))
        )
    ]
    for copy in small[:2] + copies[:2] + small[2:] + copies[2:]:
        copy.start()
    small[0].wait()
    small[1].wait()

    seq_place = lax.axis_index("seq")
    first = (seq_place * TOK).astype(f32)
    dest_row = dests[...].astype(f32)
    eye = iota((IMG, IMG), 0) == iota((IMG, IMG), 1)
    dest_col = jnp.sum(jnp.where(eye, dest_row, 0.0), axis=1, keepdims=True)
    hi_row = jnp.floor(dest_row * (1.0 / TOK))
    hi_col = jnp.floor(dest_col * (1.0 / TOK))
    lo_row = dest_row - TOK * hi_row
    lo_col = dest_col - TOK * hi_col

    index_col = jnp.concatenate([first + fiota((TOK, 1), 0), dest_col], axis=0)
    start_col = jnp.zeros((ROWS, 1), f32)
    begin = jnp.int32(0)
    for d in range(DOCS):
        begin_f = begin.astype(f32)
        start_col = jnp.where(index_col >= begin_f, begin_f, start_col)
        begin = begin + docs_ref[d]
    starts[...] = jnp.broadcast_to(start_col[:TOK], (TOK, HD))
    angles = (index_col - start_col) * invfs[...]
    cosine = jnp.cos(angles)
    sine = jnp.sin(angles)
    css[0] = cosine
    css[1] = jnp.where(iota((ROWS, HD), 1) < HD // 2, -sine, sine)

    earlier = iota((IMG, IMG), 0) < iota((IMG, IMG), 1)
    later = iota((IMG, IMG), 0) > iota((IMG, IMG), 1)
    same = hi_col == hi_row
    rank_row = jnp.sum(jnp.where(same & earlier, 1.0, 0.0), axis=0, keepdims=True)
    rank_col = jnp.sum(jnp.where(same & later, 1.0, 0.0), axis=1, keepdims=True)
    count = N_SEQ * TAIL
    line = iota((count, IMG), 0)
    here = hi_row == (line // TAIL).astype(f32)
    slot = (line % TAIL).astype(f32)
    offsets = jnp.where(here & (slot == 14.0), lo_row + 1.0, 0.0).astype(bf16)
    lane = iota((IMG, HD), 1)
    ranked = jnp.where((rank_col == lane.astype(f32)) & (lane < CAP), 1.0, 0.0).astype(bf16)
    tail = jnp.dot(offsets, ranked, preferred_element_type=f32)
    spread = (lane % 64) == iota((IMG, HD), 0)
    unused = (iota((1, HD), 1) % 64) >= IMG
    hi_two = jnp.where(unused, 99.0, jnp.sum(jnp.where(spread, hi_col, 0.0), axis=0, keepdims=True))
    lo_two = jnp.sum(jnp.where(spread, lo_col, 0.0), axis=0, keepdims=True)
    wide_slot = iota((count, HD), 0) % TAIL
    tail = tail + jnp.where(wide_slot == 12, hi_two, jnp.where(wide_slot == 13, lo_two, 0.0))

    outs = [
        pltpu.make_async_copy(css, cs_hbm, out_sems.at[0]),
        pltpu.make_async_copy(starts, start_hbm, out_sems.at[1]),
        pltpu.make_async_copy(kv_ref, kv_hbm, out_sems.at[2]),
        pltpu.make_async_copy(q_ref, q_hbm, out_sems.at[3]),
        pltpu.make_async_copy(tails, tail_hbm, out_sems.at[4]),
    ]
    outs[0].start()
    outs[1].start()

    inverse = []
    for i, rows in enumerate((pl.ds(0, TOK), pl.ds(TOK, IMG))):
        copies[i].wait()
        squares = jnp.zeros((rows.size, HD), f32)
        for c in range(width // HD):
            wide = xs[rows, c * HD : (c + 1) * HD].astype(f32)
            squares = squares + wide * wide
        inverse.append(
            lax.rsqrt(jnp.sum(squares, axis=1, keepdims=True) * (1.0 / width) + norm_eps)
        )
    inverse = jnp.concatenate(inverse, axis=0)

    for copy in small[2:] + copies[2:4]:
        copy.wait()
    queries = jnp.broadcast_to(bqs[...].astype(f32).reshape(1, 2 * HD), (ROWS, 2 * HD))
    kv = jnp.zeros((ROWS, 64), f32)
    for copy in copies[4:]:
        copy.wait()
    for c in range(KCH):
        part = pl.ds(c * step, step)
        gain = gains[part].astype(f32).reshape(1, step)
        normed = (xs[:, part].astype(f32) * inverse * gain).astype(bf16)
        kv = kv + dot_t(normed, wkvs[:, part])
        queries = queries + jnp.dot(normed, wqs[part, :], preferred_element_type=f32)

    kv = jnp.concatenate([kv, jnp.zeros((ROWS, 64), f32)], axis=1)
    kv = jnp.concatenate([kv, jnp.zeros((256 - ROWS, 128), f32)], axis=0)
    kv_t = jnp.transpose(kv)
    eye8 = iota((8, 8), 0) == iota((8, 8), 1)
    for g in range(4):
        key = kv_t[8 * g : 8 * g + 8].astype(bf16)
        bias_row = bvs[g : g + 1, :].astype(f32)
        bias = jnp.sum(jnp.where(eye8, bias_row, 0.0), axis=1, keepdims=True)
        value = (kv_t[32 + 8 * g : 40 + 8 * g] + bias).astype(bf16)
        for j in range(2):
            kv_ref[4 * g + 2 * j] = key
            kv_ref[4 * g + 2 * j + 1] = value
    outs[2].start()

    cosine = css[0]
    sine = css[1]
    for e in range(2):
        v = queries[:, e * HD : (e + 1) * HD]
        v = (v * cosine + pltpu.roll(v, HD // 2, 1) * sine).astype(bf16)
        q_ref[e] = v[:TOK]
        pick = here & (rank_row == slot - CAP * e) & (slot >= CAP * e) & (slot < CAP * e + CAP)
        tail = tail + jnp.dot(
            jnp.where(pick, 1.0, 0.0).astype(bf16), v[TOK:], preferred_element_type=f32
        )
    outs[3].start()
    tails[...] = tail.astype(bf16).reshape(N_SEQ, TAIL, HD)
    outs[4].start()
    for out in outs:
        out.wait()


def panel_kernel(kv_ref, cs_ref, tail_ref, pay_ref):
    is_key = lax.axis_index("head") % 2 == 0
    panel = jnp.transpose(kv_ref[...].astype(f32).reshape(HD, 256))[:ROWS]
    cosine = jnp.where(is_key, cs_ref[0], 1.0)
    sine = jnp.where(is_key, cs_ref[1], 0.0)
    panel = (panel * cosine + pltpu.roll(panel, HD // 2, 1) * sine).astype(bf16)
    for p in range(N_SEQ):
        pay_ref[p, 0:ROWS, :] = panel
        pay_ref[p, ROWS:PAY, :] = tail_ref[p]


def place_kernel(q_ref, mine_ref, first_ref, mask_ref, merged_ref, where_ref, start_ref):
    start_ref[...] = first_ref[...]
    tails = mine_ref[:, ROWS:PAY, :].astype(f32)
    hi_all = tails[:, 12, :]
    lo_all = tails[:, 13, :]
    slots = tails[:, 14, :]
    count = N_SEQ * TAIL
    owner = iota((count, N_SEQ), 0) // TAIL == iota((count, N_SEQ), 1)
    spread = jnp.dot(
        jnp.where(owner, 1.0, 0.0).astype(bf16), slots.astype(bf16), preferred_element_type=f32
    )
    line = iota((count, HD), 0) % TAIL
    lane = iota((count, HD), 1)
    flat = mine_ref[:, ROWS:PAY, :].reshape(count, HD)
    for e in range(2):
        slot = line - CAP * e
        used = (slot >= 0) & (slot < CAP)
        offset = jnp.sum(jnp.where(used & (lane == slot), spread, 0.0), axis=1, keepdims=True)
        place = jnp.where(offset == lane.astype(f32) + 1.0, 1.0, 0.0).astype(bf16)
        moved = tdot(place, flat)
        taken = tdot(place, jnp.ones((count, HD), bf16))
        merged_ref[e * TOK : (e + 1) * TOK, :] = jnp.where(taken > 0.5, moved.astype(bf16), q_ref[e])

    low_half = iota((1, HD), 1) < 64
    covered = jnp.zeros((N_SEQ, HD), f32)
    for m in range(N_SEQ // 2):
        hi = jnp.where(low_half, hi_all[2 * m : 2 * m + 1], hi_all[2 * m + 1 : 2 * m + 2])
        lo = jnp.where(low_half, lo_all[2 * m : 2 * m + 1], lo_all[2 * m + 1 : 2 * m + 2])
        hi_hot = jnp.where(hi == fiota((N_SEQ, HD), 0), 1.0, 0.0).astype(bf16)
        lo_hot = jnp.where(lo == fiota((HD, HD), 0), 1.0, 0.0).astype(bf16)
        covered = covered + dot_t(hi_hot, lo_hot)
        seen = jnp.zeros((1, HD), f32)
        for b in range(N_SEQ):
            seen = jnp.where(hi == float(b), mask_ref[0, b].astype(f32), seen)
        where_ref[N_SEQ + m : N_SEQ + m + 1, :] = jnp.where(seen > 0.5, hi * float(TOK) + lo, BIG)
    for b in range(N_SEQ):
        free = (covered[b : b + 1] < 0.5) & (mask_ref[0, b] == 1)
        where_ref[b : b + 1, :] = jnp.where(free, float(TOK * b) + fiota((1, HD), 1), BIG)


def attend_kernel(q_ref, where_ref, start_ref, mine_ref, other_ref, out_ref, scores):
    is_key = lax.axis_index("head") % 2 == 0
    first = (lax.axis_index("seq") * TOK).astype(f32)
    tiles = N_SEQ + N_SEQ // 2
    slope = math.log2(math.e) / math.sqrt(HD)

    def tile_of(ref, t):
        if t < N_SEQ:
            return ref[t, 0:TOK, :]
        m = t - N_SEQ
        return ref[2 * m : 2 * m + 2, TOK:PAY, :].reshape(HD, HD)

    def attend(keys, values):
        queries = q_ref[...]
        position = first + fiota((TOK, HD), 0)
        start = start_ref[...]
        top = jnp.full((2 * TOK, HD), NEG, f32)
        for t in range(tiles):
            where = where_ref[t : t + 1, :]
            allowed = (where <= position) & (where >= start)
            allowed = jnp.concatenate([allowed, allowed], axis=0)
            score = jnp.where(allowed, dot_t(queries, tile_of(keys, t)), NEG)
            scores[t] = score
            top = jnp.maximum(top, score)
        top = jnp.max(top, axis=1, keepdims=True)
        total = jnp.zeros((2 * TOK, HD), f32)
        mix = jnp.zeros((2 * TOK, HD), f32)
        for t in range(tiles):
            weight = jnp.exp2((scores[t] - top) * slope)
            total = total + weight
            mix = mix + jnp.dot(weight.astype(bf16), tile_of(values, t), preferred_element_type=f32)
        mix = mix / jnp.sum(total, axis=1, keepdims=True)
        out_ref[:, 0:HD] = mix[:TOK].astype(bf16)
        out_ref[:, HD : 2 * HD] = mix[TOK:].astype(bf16)

    @pl.when(is_key)
    def _():
        attend(mine_ref, other_ref)

    @pl.when(jnp.logical_not(is_key))
    def _():
        attend(other_ref, mine_ref)


def vmem():
    return pl.BlockSpec(memory_space=pltpu.VMEM)


def project_call(width):
    hbm = pl.BlockSpec(memory_space=pltpu.HBM)
    smem = pl.BlockSpec(memory_space=pltpu.SMEM)
    return pl.pallas_call(
        project_kernel,
        name="project",
        out_shape=(
            jax.ShapeDtypeStruct((2, TOK, HD), bf16),
            jax.ShapeDtypeStruct((N_HEAD, 8, 256), bf16),
            jax.ShapeDtypeStruct((N_SEQ, TAIL, HD), bf16),
            jax.ShapeDtypeStruct((2, ROWS, HD), f32),
            jax.ShapeDtypeStruct((TOK, HD), f32),
        ),
        in_specs=[hbm] * 10 + [smem],
        out_specs=(hbm,) * 5,
        scratch_shapes=[
            pltpu.VMEM((2, TOK, HD), bf16),
            pltpu.VMEM((N_HEAD, 8, 256), bf16),
            pltpu.VMEM((ROWS, width), bf16),
            pltpu.VMEM((width, 2 * HD), bf16),
            pltpu.VMEM((64, width), bf16),
            pltpu.VMEM((width,), bf16),
            pltpu.VMEM((2 * HD,), bf16),
            pltpu.VMEM((4, 8), bf16),
            pltpu.VMEM((1, IMG), jnp.int32),
            pltpu.VMEM((1, HD), f32),
            pltpu.VMEM((N_SEQ, TAIL, HD), bf16),
            pltpu.VMEM((2, ROWS, HD), f32),
            pltpu.VMEM((TOK, HD), f32),
            pltpu.SemaphoreType.DMA((4 + KCH,)),
            pltpu.SemaphoreType.DMA((5,)),
            pltpu.SemaphoreType.DMA((5,)),
        ],
        compiler_params=pltpu.CompilerParams(vmem_limit_bytes=LIMIT),
    )


def panel_call():
    return pl.pallas_call(
        panel_kernel,
        name="panel",
        out_shape=jax.ShapeDtypeStruct((N_SEQ, PAY, HD), bf16),
        in_specs=[vmem()] * 3,
        out_specs=vmem(),
        compiler_params=pltpu.CompilerParams(vmem_limit_bytes=SMALL),
    )


def body(
    embedded,
    norm_gain,
    query_weight,
    query_bias,
    key_weight,
    value_weight,
    value_bias,
    image_rows,
    image_dest,
    doc_lengths,
    block_mask,
):
    width = embedded.shape[1]
    half = np.arange(HD) % (HD // 2)
    inverse = jnp.asarray((rope_base ** (-2.0 * half / HD)).astype(np.float32)[None, :])
    smem = pl.BlockSpec(memory_space=pltpu.SMEM)
    key_t = jnp.transpose(key_weight, (1, 2, 0)).reshape(32, width)
    value_t = jnp.transpose(value_weight, (1, 2, 0)).reshape(32, width)
    queries, kv_send, tail, tables, start = project_call(width)(
        embedded, image_rows, query_weight, key_t, value_t, norm_gain, query_bias,
        value_bias, image_dest[None, :], inverse, doc_lengths,
    )
    kv_mine = lax.all_to_all(kv_send, "head", 0, 0)
    payload = panel_call()(kv_mine, tables, tail)
    mine = lax.all_to_all(payload, "seq", 0, 0)
    other = lax.ppermute(mine, "head", [(i, i ^ 1) for i in range(N_HEAD)])
    merged, where, start = pl.pallas_call(
        place_kernel,
        name="place",
        out_shape=(
            jax.ShapeDtypeStruct((2 * TOK, HD), bf16),
            jax.ShapeDtypeStruct((N_SEQ + N_SEQ // 2, HD), f32),
            jax.ShapeDtypeStruct((TOK, HD), f32),
        ),
        in_specs=[vmem()] * 3 + [smem],
        out_specs=(vmem(),) * 3,
        compiler_params=pltpu.CompilerParams(vmem_limit_bytes=SMALL),
        cost_estimate=pl.CostEstimate(flops=1 << 28, bytes_accessed=1 << 20, transcendentals=0),
    )(queries, mine, start, block_mask)
    return pl.pallas_call(
        attend_kernel,
        name="attend",
        out_shape=jax.ShapeDtypeStruct((TOK, 2 * HD), bf16),
        in_specs=[vmem()] * 5,
        out_specs=vmem(),
        scratch_shapes=[pltpu.VMEM((N_SEQ + N_SEQ // 2, 2 * TOK, HD), f32)],
        compiler_params=pltpu.CompilerParams(vmem_limit_bytes=SMALL),
    )(merged, where, start, mine, other)


def solution(mesh):
    in_specs = (
        P("seq", None),
        P(),
        P(None, "head"),
        P("head"),
        P(None, None, "head"),
        P(None, None, "head"),
        P(None, "head"),
        P("seq", None),
        P("seq"),
        P(),
        P("seq", None),
    )
    out_specs = P("seq", "head")
    return jax.shard_map(body, mesh=mesh, in_specs=in_specs, out_specs=out_specs, check_vma=False)
```

```python
import functools
import math

import jax
import jax.numpy as jnp
import numpy as np
from jax import lax
from jax.experimental import pallas as pl
from jax.experimental.pallas import tpu as pltpu
from jax.sharding import PartitionSpec as P

HD = 128
GROUP = 8
BLK = 128
CAP = 6
TOK = 128
IMG = 48
N_SEQ = 16
N_HEAD = 16
ROWS = TOK + IMG
HALF_TOK = TOK // 2
HALF_IMG = IMG // 2
KEYS = HALF_TOK + HALF_IMG
TAIL = 16
PAY = KEYS + 2 * TAIL
TILES = N_SEQ // 2 + N_SEQ // 4
DOCS = 32
KCH = 4
LIMIT = 60 << 20
SMALL = 12 << 20

rope_base = 1000000.0
norm_eps = 1e-06
BIG = 1.0e6
NEG = -1.0e30
LOW = -1.0e29

f32 = jnp.float32
bf16 = jnp.bfloat16


def iota(shape, dim):
    return lax.broadcasted_iota(jnp.int32, shape, dim)


def fiota(shape, dim):
    return iota(shape, dim).astype(f32)


def dot_t(a, b):
    return lax.dot_general(a, b, (((1,), (1,)), ((), ())), preferred_element_type=f32)


def tdot(a, b):
    return lax.dot_general(a, b, (((0,), (0,)), ((), ())), preferred_element_type=f32)


def project_kernel(
    x_hbm, img_hbm, wq_hbm, wk_hbm, wv_hbm, gain_hbm, bq_hbm, bv_hbm, dest_hbm, invf_hbm, docs_ref,
    kv_hbm, share_hbm, aux_hbm, own_hbm,
    kv_ref, share, aux, own, xs, wqs, wkvs, gains, bqs, bvs, dests, invfs, css, sems, small_sems, out_sems,
):
    width = xs.shape[1]
    step = width // KCH
    copies = [
        pltpu.make_async_copy(x_hbm, xs.at[pl.ds(0, TOK)], sems.at[0]),
        pltpu.make_async_copy(img_hbm, xs.at[pl.ds(TOK, IMG)], sems.at[1]),
        pltpu.make_async_copy(wk_hbm, wkvs.at[pl.ds(0, 32)], sems.at[2]),
        pltpu.make_async_copy(wv_hbm, wkvs.at[pl.ds(32, 32)], sems.at[3]),
    ]
    for c in range(KCH):
        part = pl.ds(c * step, step)
        copies.append(pltpu.make_async_copy(wq_hbm.at[part], wqs.at[part], sems.at[4 + c]))
    small = [
        pltpu.make_async_copy(src, dst, small_sems.at[i])
        for i, (src, dst) in enumerate(
            ((dest_hbm, dests), (invf_hbm, invfs), (gain_hbm, gains), (bq_hbm, bqs), (bv_hbm, bvs))
        )
    ]
    for copy in small[:2] + copies[:2] + small[2:] + copies[2:]:
        copy.start()
    small[0].wait()
    small[1].wait()

    seq_place = lax.axis_index("seq")
    first = (seq_place * TOK).astype(f32)
    dest_row = dests[...].astype(f32)
    eye = iota((IMG, IMG), 0) == iota((IMG, IMG), 1)
    dest_col = jnp.sum(jnp.where(eye, dest_row, 0.0), axis=1, keepdims=True)
    hi_row = jnp.floor(dest_row * (1.0 / TOK))
    hi_col = jnp.floor(dest_col * (1.0 / TOK))
    lo_row = dest_row - TOK * hi_row
    lo_col = dest_col - TOK * hi_col

    index_col = jnp.concatenate([first + fiota((TOK, 1), 0), dest_col], axis=0)
    start_col = jnp.zeros((ROWS, 1), f32)
    begin = jnp.int32(0)
    for d in range(DOCS):
        begin_f = begin.astype(f32)
        start_col = jnp.where(index_col >= begin_f, begin_f, start_col)
        begin = begin + docs_ref[d]
    own[2 * TOK :, :] = jnp.broadcast_to(start_col[:TOK], (TOK, HD))
    angles = (index_col - start_col) * invfs[...]
    cosine = jnp.cos(angles)
    sine = jnp.sin(angles)
    sine = jnp.where(iota((ROWS, HD), 1) < HD // 2, -sine, sine)
    upper = (lax.axis_index("head") // 2) % 2 == 1
    for i, table in enumerate((cosine, sine)):
        css[i] = table
        low = i * KEYS
        aux[low : low + HALF_TOK, :] = jnp.where(upper, table[HALF_TOK:TOK], table[:HALF_TOK])
        aux[low + HALF_TOK : low + KEYS, :] = jnp.where(
            upper, table[TOK + HALF_IMG :], table[TOK : TOK + HALF_IMG]
        )

    earlier = iota((IMG, IMG), 0) < iota((IMG, IMG), 1)
    later = iota((IMG, IMG), 0) > iota((IMG, IMG), 1)
    same = hi_col == hi_row
    rank_row = jnp.sum(jnp.where(same & earlier, 1.0, 0.0), axis=0, keepdims=True)
    rank_col = jnp.sum(jnp.where(same & later, 1.0, 0.0), axis=1, keepdims=True)
    count = N_SEQ * TAIL
    line = iota((count, IMG), 0)
    here = hi_row == (line // TAIL).astype(f32)
    slot = (line % TAIL).astype(f32)
    offsets = jnp.where(here & (slot == 14.0), lo_row + 1.0, 0.0).astype(bf16)
    lane = iota((IMG, HD), 1)
    ranked = jnp.where((rank_col == lane.astype(f32)) & (lane < CAP), 1.0, 0.0).astype(bf16)
    tail = jnp.dot(offsets, ranked, preferred_element_type=f32)
    skip = jnp.where(upper, HALF_IMG, 0)
    spread = (lane % 32 + skip == iota((IMG, HD), 0)) & (lane % 32 < HALF_IMG)
    unused = (iota((1, HD), 1) % 32) >= HALF_IMG
    hi_two = jnp.where(unused, 99.0, jnp.sum(jnp.where(spread, hi_col, 0.0), axis=0, keepdims=True))
    lo_two = jnp.sum(jnp.where(spread, lo_col, 0.0), axis=0, keepdims=True)
    wide_slot = iota((count, HD), 0) % TAIL
    tail = tail + jnp.where(wide_slot == 12, hi_two, jnp.where(wide_slot == 13, lo_two, 0.0))

    outs = [
        pltpu.make_async_copy(kv_ref, kv_hbm, out_sems.at[0]),
        pltpu.make_async_copy(share, share_hbm, out_sems.at[1]),
        pltpu.make_async_copy(own, own_hbm, out_sems.at[2]),
        pltpu.make_async_copy(aux, aux_hbm, out_sems.at[3]),
    ]

    inverse = []
    for i, rows in enumerate((pl.ds(0, TOK), pl.ds(TOK, IMG))):
        copies[i].wait()
        squares = jnp.zeros((rows.size, HD), f32)
        for c in range(width // HD):
            wide = xs[rows, c * HD : (c + 1) * HD].astype(f32)
            squares = squares + wide * wide
        inverse.append(
            lax.rsqrt(jnp.sum(squares, axis=1, keepdims=True) * (1.0 / width) + norm_eps)
        )
    inverse = jnp.concatenate(inverse, axis=0)

    for copy in small[2:] + copies[2:4]:
        copy.wait()
    queries = jnp.broadcast_to(bqs[...].astype(f32).reshape(1, 2 * HD), (ROWS, 2 * HD))
    kv = jnp.zeros((ROWS, 64), f32)
    for copy in copies[4:]:
        copy.wait()
    for c in range(KCH):
        part = pl.ds(c * step, step)
        gain = gains[part].astype(f32).reshape(1, step)
        normed = (xs[:, part].astype(f32) * inverse * gain).astype(bf16)
        kv = kv + dot_t(normed, wkvs[:, part])
        queries = queries + jnp.dot(normed, wqs[part, :], preferred_element_type=f32)

    kv = jnp.concatenate([kv, jnp.zeros((ROWS, 64), f32)], axis=1)
    eye8 = iota((8, 8), 0) == iota((8, 8), 1)
    for j in range(2):
        kv_t = jnp.transpose(
            jnp.concatenate(
                [
                    kv[HALF_TOK * j : HALF_TOK * (j + 1)],
                    kv[TOK + HALF_IMG * j : TOK + HALF_IMG * (j + 1)],
                    jnp.zeros((HD - KEYS, HD), f32),
                ],
                axis=0,
            )
        )
        for g in range(4):
            bias_row = bvs[g : g + 1, :].astype(f32)
            bias = jnp.sum(jnp.where(eye8, bias_row, 0.0), axis=1, keepdims=True)
            kv_ref[4 * g + 2 * j] = kv_t[8 * g : 8 * g + 8].astype(bf16)
            kv_ref[4 * g + 2 * j + 1] = (kv_t[32 + 8 * g : 40 + 8 * g] + bias).astype(bf16)
    outs[0].start()

    cosine = css[0]
    sine = css[1]
    for e in range(2):
        v = queries[:, e * HD : (e + 1) * HD]
        v = (v * cosine + pltpu.roll(v, HD // 2, 1) * sine).astype(bf16)
        share[e * TOK : (e + 1) * TOK, :] = v[:TOK]
        own[e * TOK : (e + 1) * TOK, :] = v[:TOK].astype(f32)
        pick = here & (rank_row == slot - CAP * e) & (slot >= CAP * e) & (slot < CAP * e + CAP)
        tail = tail + jnp.dot(
            jnp.where(pick, 1.0, 0.0).astype(bf16), v[TOK:], preferred_element_type=f32
        )
    outs[2].start()
    share[2 * TOK :, :] = tail.astype(bf16)
    outs[1].start()
    aux[2 * KEYS :, :] = tail
    outs[3].start()
    for out in outs:
        out.wait()


def panel_kernel(kv_ref, aux_ref, share_ref, pay_ref):
    is_key = lax.axis_index("head") % 2 == 0
    panel = jnp.transpose(kv_ref[...].astype(f32).reshape(HD, HD))[:KEYS]
    cosine = jnp.where(is_key, aux_ref[0:KEYS, :], 1.0)
    sine = jnp.where(is_key, aux_ref[KEYS : 2 * KEYS, :], 0.0)
    panel = (panel * cosine + pltpu.roll(panel, HD // 2, 1) * sine).astype(bf16)
    for p in range(N_SEQ):
        low = 2 * KEYS + TAIL * p
        pay_ref[p, 0:KEYS, :] = panel
        pay_ref[p, KEYS : KEYS + TAIL, :] = aux_ref[low : low + TAIL, :].astype(bf16)
        low = 2 * TOK + TAIL * p
        pay_ref[p, KEYS + TAIL : PAY, :] = share_ref[low : low + TAIL, :]


def place_kernel(own_ref, share_ref, mine_ref, mask_ref, merged_ref, where_ref, start_ref):
    start_ref[...] = own_ref[2 * TOK :, :]
    tails = mine_ref[:, KEYS:PAY, :].astype(f32)
    slots = tails[:, 14, :]
    count = N_SEQ * TAIL
    owner = iota((count, N_SEQ), 0) // TAIL == iota((count, N_SEQ), 1)
    spread = jnp.dot(
        jnp.where(owner, 1.0, 0.0).astype(bf16), slots.astype(bf16), preferred_element_type=f32
    )
    line = iota((count, HD), 0) % TAIL
    lane = iota((count, HD), 1)
    flats = [tails[:, c * TAIL : (c + 1) * TAIL, :].reshape(count, HD).astype(bf16) for c in range(2)]
    for e in range(2):
        slot = line - CAP * e
        used = (slot >= 0) & (slot < CAP)
        offset = jnp.sum(jnp.where(used & (lane == slot), spread, 0.0), axis=1, keepdims=True)
        place = jnp.where(offset == lane.astype(f32) + 1.0, 1.0, 0.0).astype(bf16)
        taken = tdot(place, jnp.ones((count, HD), bf16)) > 0.5
        span = slice(e * TOK, (e + 1) * TOK)
        merged_ref[span, :] = jnp.where(taken, tdot(place, flats[0]), own_ref[span, :]).astype(bf16)
        moved = jnp.where(taken, tdot(place, flats[1]), share_ref[span, :].astype(f32))
        merged_ref[(2 + e) * TOK : (3 + e) * TOK, :] = moved.astype(bf16)

    lane = iota((1, HD), 1)

    def four(rows, m):
        row = rows[4 * m + 3 : 4 * m + 4]
        for i in (2, 1, 0):
            row = jnp.where(lane < 32 * (i + 1), rows[4 * m + i : 4 * m + i + 1], row)
        return row

    covered = jnp.zeros((N_SEQ, HD), f32)
    for c in range(2):
        hi_all = tails[:, c * TAIL + 12, :]
        lo_all = tails[:, c * TAIL + 13, :]
        for m in range(N_SEQ // 4):
            hi = four(hi_all, m)
            lo = four(lo_all, m)
            hi_hot = jnp.where(hi == fiota((N_SEQ, HD), 0), 1.0, 0.0).astype(bf16)
            lo_hot = jnp.where(lo == fiota((HD, HD), 0), 1.0, 0.0).astype(bf16)
            covered = covered + dot_t(hi_hot, lo_hot)
            if c == 0:
                seen = jnp.zeros((1, HD), f32)
                for b in range(N_SEQ):
                    seen = jnp.where(hi == float(b), mask_ref[0, b].astype(f32), seen)
                at = N_SEQ // 2 + m
                where_ref[at : at + 1, :] = jnp.where(seen > 0.5, hi * float(TOK) + lo, BIG)
    upper = (lax.axis_index("head") // 2) % 2 == 1
    turned = pltpu.roll(covered, HALF_TOK, 1)
    near = jnp.where(upper, turned, covered)
    far = jnp.where(upper, covered, turned)
    base = (lane % HALF_TOK).astype(f32) + jnp.where(upper, float(HALF_TOK), 0.0)
    for m in range(N_SEQ // 2):
        left = lane < HALF_TOK
        taken = jnp.where(left, near[2 * m : 2 * m + 1], far[2 * m + 1 : 2 * m + 2])
        seen = jnp.where(left, mask_ref[0, 2 * m], mask_ref[0, 2 * m + 1])
        position = base + jnp.where(left, float(TOK * 2 * m), float(TOK * (2 * m + 1)))
        where_ref[m : m + 1, :] = jnp.where((taken < 0.5) & (seen == 1), position, BIG)


def attend_kernel(q_ref, where_ref, start_ref, mine_ref, other_ref, keep_ref, send_ref, scores):
    is_key = lax.axis_index("head") % 2 == 0
    first = (lax.axis_index("seq") * TOK).astype(f32)
    slope = math.log2(math.e) / math.sqrt(HD)

    def tile_of(ref, t):
        if t < N_SEQ // 2:
            return ref[2 * t : 2 * t + 2, 0:HALF_TOK, :].reshape(HD, HD)
        m = t - N_SEQ // 2
        return ref[4 * m : 4 * m + 4, HALF_TOK : HALF_TOK + 32, :].reshape(HD, HD)

    def attend(keys, values):
        queries = q_ref[...]
        position = first + fiota((TOK, HD), 0)
        start = start_ref[...]
        top = jnp.full((4 * TOK, HD), NEG, f32)
        for t in range(TILES):
            where = where_ref[t : t + 1, :]
            allowed = (where <= position) & (where >= start)
            allowed = jnp.concatenate([allowed] * 4, axis=0)
            score = jnp.where(allowed, dot_t(queries, tile_of(keys, t)), NEG)
            scores[t] = score
            top = jnp.maximum(top, score)
        top = jnp.maximum(jnp.max(top, axis=1, keepdims=True), LOW)
        total = jnp.zeros((4 * TOK, HD), f32)
        mix = jnp.zeros((4 * TOK, HD), f32)
        for t in range(TILES):
            weight = jnp.exp2((scores[t] - top) * slope)
            total = total + weight
            mix = mix + jnp.dot(weight.astype(bf16), tile_of(values, t), preferred_element_type=f32)
        total = jnp.sum(total, axis=1, keepdims=True)
        mine = 2 * TOK
        keep_ref[0] = mix[:mine]
        keep_ref[1] = jnp.broadcast_to(top[:mine], (mine, HD))
        keep_ref[2] = jnp.broadcast_to(total[:mine], (mine, HD))
        send_ref[0:mine, :] = (mix[mine:] / jnp.maximum(total[mine:], 1.0e-30)).astype(bf16)
        rows = []
        for column in (top[mine:], total[mine:]):
            for e in range(2):
                part = jnp.broadcast_to(column[e * TOK : (e + 1) * TOK], (TOK, HD))
                left = jnp.transpose(part)[0:1]
                for _ in range(3):
                    piece = left.astype(bf16).astype(f32)
                    rows.append(piece)
                    left = left - piece
        rows.append(jnp.zeros((4, HD), f32))
        send_ref[mine:, :] = jnp.concatenate(rows, axis=0).astype(bf16)

    @pl.when(is_key)
    def _():
        attend(mine_ref, other_ref)

    @pl.when(jnp.logical_not(is_key))
    def _():
        attend(other_ref, mine_ref)


def combine_kernel(keep_ref, come_ref, out_ref):
    slope = math.log2(math.e) / math.sqrt(HD)
    pieces = come_ref[2 * TOK :, :].astype(f32)

    def column(i):
        row = pieces[3 * i : 3 * i + 1] + pieces[3 * i + 1 : 3 * i + 2] + pieces[3 * i + 2 : 3 * i + 3]
        return jnp.transpose(jnp.broadcast_to(row, (TOK, HD)))

    for e in range(2):
        span = slice(e * TOK, (e + 1) * TOK)
        top_near = keep_ref[1, span, :]
        top_far = column(e)
        top = jnp.maximum(top_near, top_far)
        near = jnp.exp2((top_near - top) * slope)
        far = jnp.exp2((top_far - top) * slope) * column(2 + e)
        mix = keep_ref[0, span, :] * near + come_ref[span, :].astype(f32) * far
        out_ref[:, e * HD : (e + 1) * HD] = (mix / (keep_ref[2, span, :] * near + far)).astype(bf16)


def vmem():
    return pl.BlockSpec(memory_space=pltpu.VMEM)


def small_params():
    return pltpu.CompilerParams(vmem_limit_bytes=SMALL)


def project_call(width):
    hbm = pl.BlockSpec(memory_space=pltpu.HBM)
    smem = pl.BlockSpec(memory_space=pltpu.SMEM)
    outputs = [
        ((N_HEAD, 8, HD), bf16),
        ((2 * TOK + N_SEQ * TAIL, HD), bf16),
        ((2 * KEYS + N_SEQ * TAIL, HD), f32),
        ((3 * TOK, HD), f32),
    ]
    return pl.pallas_call(
        project_kernel,
        name="project",
        out_shape=tuple(jax.ShapeDtypeStruct(shape, dtype) for shape, dtype in outputs),
        in_specs=[hbm] * 10 + [smem],
        out_specs=(hbm,) * 4,
        scratch_shapes=[pltpu.VMEM(shape, dtype) for shape, dtype in outputs]
        + [
            pltpu.VMEM((ROWS, width), bf16),
            pltpu.VMEM((width, 2 * HD), bf16),
            pltpu.VMEM((64, width), bf16),
            pltpu.VMEM((width,), bf16),
            pltpu.VMEM((2 * HD,), bf16),
            pltpu.VMEM((4, 8), bf16),
            pltpu.VMEM((1, IMG), jnp.int32),
            pltpu.VMEM((1, HD), f32),
            pltpu.VMEM((2, ROWS, HD), f32),
            pltpu.SemaphoreType.DMA((4 + KCH,)),
            pltpu.SemaphoreType.DMA((5,)),
            pltpu.SemaphoreType.DMA((4,)),
        ],
        compiler_params=pltpu.CompilerParams(vmem_limit_bytes=LIMIT),
    )


def panel_call():
    return pl.pallas_call(
        panel_kernel,
        name="panel",
        out_shape=jax.ShapeDtypeStruct((N_SEQ, PAY, HD), bf16),
        in_specs=[vmem()] * 3,
        out_specs=vmem(),
        compiler_params=small_params(),
    )


def body(
    embedded,
    norm_gain,
    query_weight,
    query_bias,
    key_weight,
    value_weight,
    value_bias,
    image_rows,
    image_dest,
    doc_lengths,
    block_mask,
):
    width = embedded.shape[1]
    half = np.arange(HD) % (HD // 2)
    inverse = jnp.asarray((rope_base ** (-2.0 * half / HD)).astype(np.float32)[None, :])
    smem = pl.BlockSpec(memory_space=pltpu.SMEM)
    key_t = jnp.transpose(key_weight, (1, 2, 0)).reshape(32, width)
    value_t = jnp.transpose(value_weight, (1, 2, 0)).reshape(32, width)
    kv_send, share, aux, own = project_call(width)(
        embedded, image_rows, query_weight, key_t, value_t, norm_gain, query_bias,
        value_bias, image_dest[None, :], inverse, doc_lengths,
    )
    chip_swap = [(i, i ^ 2) for i in range(N_HEAD)]
    core_swap = [(i, i ^ 1) for i in range(N_HEAD)]
    shared = lax.ppermute(share, "head", chip_swap)
    kv_mine = lax.all_to_all(kv_send, "head", 0, 0)
    payload = panel_call()(kv_mine, aux, shared)
    mine = lax.all_to_all(payload, "seq", 0, 0)
    other = lax.ppermute(mine, "head", core_swap)
    merged, where, start = pl.pallas_call(
        place_kernel,
        name="place",
        out_shape=(
            jax.ShapeDtypeStruct((4 * TOK, HD), bf16),
            jax.ShapeDtypeStruct((TILES, HD), f32),
            jax.ShapeDtypeStruct((TOK, HD), f32),
        ),
        in_specs=[vmem()] * 3 + [smem],
        out_specs=(vmem(),) * 3,
        compiler_params=small_params(),
        cost_estimate=pl.CostEstimate(flops=1 << 28, bytes_accessed=1 << 20, transcendentals=0),
    )(own, shared, mine, block_mask)
    keep, send = pl.pallas_call(
        attend_kernel,
        name="attend",
        out_shape=(
            jax.ShapeDtypeStruct((3, 2 * TOK, HD), f32),
            jax.ShapeDtypeStruct((2 * TOK + 16, HD), bf16),
        ),
        in_specs=[vmem()] * 5,
        out_specs=(vmem(), vmem()),
        scratch_shapes=[pltpu.VMEM((TILES, 4 * TOK, HD), f32)],
        compiler_params=small_params(),
    )(merged, where, start, mine, other)
    come = lax.ppermute(send, "head", chip_swap)
    return pl.pallas_call(
        combine_kernel,
        name="combine",
        out_shape=jax.ShapeDtypeStruct((TOK, 2 * HD), bf16),
        in_specs=[vmem()] * 2,
        out_specs=vmem(),
        compiler_params=small_params(),
    )(keep, come)


def solution(mesh):
    in_specs = (
        P("seq", None),
        P(),
        P(None, "head"),
        P("head"),
        P(None, None, "head"),
        P(None, None, "head"),
        P(None, "head"),
        P("seq", None),
        P("seq"),
        P(),
        P("seq", None),
    )
    out_specs = P("seq", "head")
    return jax.shard_map(body, mesh=mesh, in_specs=in_specs, out_specs=out_specs, check_vma=False)
```

```python
import functools
import math

import jax
import jax.numpy as jnp
import numpy as np
from jax import lax
from jax.experimental import pallas as pl
from jax.experimental.pallas import tpu as pltpu
from jax.sharding import PartitionSpec as P

HD = 128
GROUP = 8
BLK = 128
CAP = 6
TOK = 128
IMG = 48
N_SEQ = 16
N_HEAD = 16
ROWS = TOK + IMG
HALF_TOK = TOK // 2
HALF_IMG = IMG // 2
KEYS = HALF_TOK + HALF_IMG
TAIL = 16
PAY = KEYS + 2 * TAIL
TILES = N_SEQ // 2 + N_SEQ // 4
DOCS = 32
KCH = 4
LIMIT = 60 << 20
SMALL = 12 << 20

rope_base = 1000000.0
norm_eps = 1e-06
BIG = 1.0e6
NEG = -1.0e30
LOW = -1.0e29

f32 = jnp.float32
bf16 = jnp.bfloat16


def iota(shape, dim):
    return lax.broadcasted_iota(jnp.int32, shape, dim)


def fiota(shape, dim):
    return iota(shape, dim).astype(f32)


def dot_t(a, b):
    return lax.dot_general(a, b, (((1,), (1,)), ((), ())), preferred_element_type=f32)


def tdot(a, b):
    return lax.dot_general(a, b, (((0,), (0,)), ((), ())), preferred_element_type=f32)


def project_kernel(
    x_hbm, img_hbm, wq_hbm, wk_hbm, wv_hbm, gain_hbm, bq_hbm, bv_hbm, dest_hbm, invf_hbm, docs_hbm,
    kv_ref, share, aux, own,
    xs, wqs, wkvs, gains, bqs, bvs, dests, invfs, docs_ref, css, sems, small_sems,
):
    width = xs.shape[1]
    step = width // KCH
    copies = [
        pltpu.make_async_copy(x_hbm, xs.at[pl.ds(0, TOK)], sems.at[0]),
        pltpu.make_async_copy(img_hbm, xs.at[pl.ds(TOK, IMG)], sems.at[1]),
        pltpu.make_async_copy(wk_hbm, wkvs.at[pl.ds(0, 32)], sems.at[2]),
        pltpu.make_async_copy(wv_hbm, wkvs.at[pl.ds(32, 32)], sems.at[3]),
    ]
    for c in range(KCH):
        part = pl.ds(c * step, step)
        copies.append(pltpu.make_async_copy(wq_hbm.at[part], wqs.at[part], sems.at[4 + c]))
    small = [
        pltpu.make_async_copy(src, dst, small_sems.at[i])
        for i, (src, dst) in enumerate(
            ((docs_hbm, docs_ref), (dest_hbm, dests), (invf_hbm, invfs), (gain_hbm, gains), (bq_hbm, bqs), (bv_hbm, bvs))
        )
    ]
    for copy in small[:3] + copies[:2] + small[3:] + copies[2:]:
        copy.start()
    inverse = []
    for i, rows in enumerate((pl.ds(0, TOK), pl.ds(TOK, IMG))):
        copies[i].wait()
        squares = jnp.zeros((rows.size, HD), f32)
        for c in range(width // HD):
            wide = xs[rows, c * HD : (c + 1) * HD].astype(f32)
            squares = squares + wide * wide
        inverse.append(
            lax.rsqrt(jnp.sum(squares, axis=1, keepdims=True) * (1.0 / width) + norm_eps)
        )
    inverse = jnp.concatenate(inverse, axis=0)

    for copy in small[:3]:
        copy.wait()

    seq_place = lax.axis_index("seq")
    first = (seq_place * TOK).astype(f32)
    dest_row = dests[...].astype(f32)
    eye = iota((IMG, IMG), 0) == iota((IMG, IMG), 1)
    dest_col = jnp.sum(jnp.where(eye, dest_row, 0.0), axis=1, keepdims=True)
    hi_row = jnp.floor(dest_row * (1.0 / TOK))
    hi_col = jnp.floor(dest_col * (1.0 / TOK))
    lo_row = dest_row - TOK * hi_row
    lo_col = dest_col - TOK * hi_col

    index_col = jnp.concatenate([first + fiota((TOK, 1), 0), dest_col], axis=0)
    start_col = jnp.zeros((ROWS, 1), f32)
    begin = jnp.int32(0)
    for d in range(DOCS):
        begin_f = begin.astype(f32)
        start_col = jnp.where(index_col >= begin_f, begin_f, start_col)
        begin = begin + docs_ref[d]
    own[2 * TOK :, :] = jnp.broadcast_to(start_col[:TOK], (TOK, HD))
    angles = (index_col - start_col) * invfs[...]
    cosine = jnp.cos(angles)
    sine = jnp.sin(angles)
    sine = jnp.where(iota((ROWS, HD), 1) < HD // 2, -sine, sine)
    upper = (lax.axis_index("head") // 2) % 2 == 1
    for i, table in enumerate((cosine, sine)):
        css[i] = table
        low = i * KEYS
        aux[low : low + HALF_TOK, :] = jnp.where(upper, table[HALF_TOK:TOK], table[:HALF_TOK])
        aux[low + HALF_TOK : low + KEYS, :] = jnp.where(
            upper, table[TOK + HALF_IMG :], table[TOK : TOK + HALF_IMG]
        )

    earlier = iota((IMG, IMG), 0) < iota((IMG, IMG), 1)
    later = iota((IMG, IMG), 0) > iota((IMG, IMG), 1)
    same = hi_col == hi_row
    rank_row = jnp.sum(jnp.where(same & earlier, 1.0, 0.0), axis=0, keepdims=True)
    rank_col = jnp.sum(jnp.where(same & later, 1.0, 0.0), axis=1, keepdims=True)
    count = N_SEQ * TAIL
    line = iota((count, IMG), 0)
    here = hi_row == (line // TAIL).astype(f32)
    slot = (line % TAIL).astype(f32)
    offsets = jnp.where(here & (slot == 14.0), lo_row + 1.0, 0.0).astype(bf16)
    lane = iota((IMG, HD), 1)
    ranked = jnp.where((rank_col == lane.astype(f32)) & (lane < CAP), 1.0, 0.0).astype(bf16)
    tail = jnp.dot(offsets, ranked, preferred_element_type=f32)
    skip = jnp.where(upper, HALF_IMG, 0)
    spread = (lane % 32 + skip == iota((IMG, HD), 0)) & (lane % 32 < HALF_IMG)
    unused = (iota((1, HD), 1) % 32) >= HALF_IMG
    hi_two = jnp.where(unused, 99.0, jnp.sum(jnp.where(spread, hi_col, 0.0), axis=0, keepdims=True))
    lo_two = jnp.sum(jnp.where(spread, lo_col, 0.0), axis=0, keepdims=True)
    wide_slot = iota((count, HD), 0) % TAIL
    tail = tail + jnp.where(wide_slot == 12, hi_two, jnp.where(wide_slot == 13, lo_two, 0.0))

    for copy in small[3:] + copies[2:4]:
        copy.wait()
    queries = jnp.broadcast_to(bqs[...].astype(f32).reshape(1, 2 * HD), (ROWS, 2 * HD))
    kv = jnp.zeros((ROWS, 64), f32)
    for c in range(KCH):
        if c % 2 == 0:
            copies[4 + c].wait()
            copies[5 + c].wait()
        part = pl.ds(c * step, step)
        gain = gains[part].astype(f32).reshape(1, step)
        normed = (xs[:, part].astype(f32) * inverse * gain).astype(bf16)
        kv = kv + dot_t(normed, wkvs[:, part])
        queries = queries + jnp.dot(normed, wqs[part, :], preferred_element_type=f32)

    kv = jnp.concatenate([kv, jnp.zeros((ROWS, 64), f32)], axis=1)
    eye8 = iota((8, 8), 0) == iota((8, 8), 1)
    for j in range(2):
        kv_t = jnp.transpose(
            jnp.concatenate(
                [
                    kv[HALF_TOK * j : HALF_TOK * (j + 1)],
                    kv[TOK + HALF_IMG * j : TOK + HALF_IMG * (j + 1)],
                    jnp.zeros((HD - KEYS, HD), f32),
                ],
                axis=0,
            )
        )
        for g in range(4):
            bias_row = bvs[g : g + 1, :].astype(f32)
            bias = jnp.sum(jnp.where(eye8, bias_row, 0.0), axis=1, keepdims=True)
            kv_ref[4 * g + 2 * j] = kv_t[8 * g : 8 * g + 8].astype(bf16)
            kv_ref[4 * g + 2 * j + 1] = (kv_t[32 + 8 * g : 40 + 8 * g] + bias).astype(bf16)

    cosine = css[0]
    sine = css[1]
    for e in range(2):
        v = queries[:, e * HD : (e + 1) * HD]
        v = (v * cosine + pltpu.roll(v, HD // 2, 1) * sine).astype(bf16)
        share[e * TOK : (e + 1) * TOK, :] = v[:TOK]
        own[e * TOK : (e + 1) * TOK, :] = v[:TOK].astype(f32)
        pick = here & (rank_row == slot - CAP * e) & (slot >= CAP * e) & (slot < CAP * e + CAP)
        tail = tail + jnp.dot(
            jnp.where(pick, 1.0, 0.0).astype(bf16), v[TOK:], preferred_element_type=f32
        )
    share[2 * TOK :, :] = tail.astype(bf16)
    aux[2 * KEYS :, :] = tail


def panel_kernel(kv_ref, aux_ref, share_ref, pay_ref):
    is_key = lax.axis_index("head") % 2 == 0
    panel = jnp.transpose(kv_ref[...].astype(f32).reshape(HD, HD))[:KEYS]
    cosine = jnp.where(is_key, aux_ref[0:KEYS, :], 1.0)
    sine = jnp.where(is_key, aux_ref[KEYS : 2 * KEYS, :], 0.0)
    panel = (panel * cosine + pltpu.roll(panel, HD // 2, 1) * sine).astype(bf16)
    for p in range(N_SEQ):
        low = 2 * KEYS + TAIL * p
        pay_ref[p, 0:KEYS, :] = panel
        pay_ref[p, KEYS : KEYS + TAIL, :] = aux_ref[low : low + TAIL, :].astype(bf16)
        low = 2 * TOK + TAIL * p
        pay_ref[p, KEYS + TAIL : PAY, :] = share_ref[low : low + TAIL, :]


def place_kernel(own_ref, share_ref, mine_ref, mask_ref, merged_ref, where_ref, start_ref):
    start_ref[...] = own_ref[2 * TOK :, :]
    tails = mine_ref[:, KEYS:PAY, :].astype(f32)
    slots = tails[:, 14, :]
    count = N_SEQ * TAIL
    owner = iota((count, N_SEQ), 0) // TAIL == iota((count, N_SEQ), 1)
    spread = jnp.dot(
        jnp.where(owner, 1.0, 0.0).astype(bf16), slots.astype(bf16), preferred_element_type=f32
    )
    line = iota((count, HD), 0) % TAIL
    lane = iota((count, HD), 1)
    flats = [tails[:, c * TAIL : (c + 1) * TAIL, :].reshape(count, HD).astype(bf16) for c in range(2)]
    for e in range(2):
        slot = line - CAP * e
        used = (slot >= 0) & (slot < CAP)
        offset = jnp.sum(jnp.where(used & (lane == slot), spread, 0.0), axis=1, keepdims=True)
        place = jnp.where(offset == lane.astype(f32) + 1.0, 1.0, 0.0).astype(bf16)
        taken = tdot(place, jnp.ones((count, HD), bf16)) > 0.5
        span = slice(e * TOK, (e + 1) * TOK)
        merged_ref[span, :] = jnp.where(taken, tdot(place, flats[0]), own_ref[span, :]).astype(bf16)
        moved = jnp.where(taken, tdot(place, flats[1]), share_ref[span, :].astype(f32))
        merged_ref[(2 + e) * TOK : (3 + e) * TOK, :] = moved.astype(bf16)

    lane = iota((1, HD), 1)

    def four(rows, m):
        row = rows[4 * m + 3 : 4 * m + 4]
        for i in (2, 1, 0):
            row = jnp.where(lane < 32 * (i + 1), rows[4 * m + i : 4 * m + i + 1], row)
        return row

    covered = jnp.zeros((N_SEQ, HD), f32)
    for c in range(2):
        hi_all = tails[:, c * TAIL + 12, :]
        lo_all = tails[:, c * TAIL + 13, :]
        for m in range(N_SEQ // 4):
            hi = four(hi_all, m)
            lo = four(lo_all, m)
            hi_hot = jnp.where(hi == fiota((N_SEQ, HD), 0), 1.0, 0.0).astype(bf16)
            lo_hot = jnp.where(lo == fiota((HD, HD), 0), 1.0, 0.0).astype(bf16)
            covered = covered + dot_t(hi_hot, lo_hot)
            if c == 0:
                seen = jnp.zeros((1, HD), f32)
                for b in range(N_SEQ):
                    seen = jnp.where(hi == float(b), mask_ref[0, b].astype(f32), seen)
                at = N_SEQ // 2 + m
                where_ref[at : at + 1, :] = jnp.where(seen > 0.5, hi * float(TOK) + lo, BIG)
    upper = (lax.axis_index("head") // 2) % 2 == 1
    turned = pltpu.roll(covered, HALF_TOK, 1)
    near = jnp.where(upper, turned, covered)
    far = jnp.where(upper, covered, turned)
    base = (lane % HALF_TOK).astype(f32) + jnp.where(upper, float(HALF_TOK), 0.0)
    for m in range(N_SEQ // 2):
        left = lane < HALF_TOK
        taken = jnp.where(left, near[2 * m : 2 * m + 1], far[2 * m + 1 : 2 * m + 2])
        seen = jnp.where(left, mask_ref[0, 2 * m], mask_ref[0, 2 * m + 1])
        position = base + jnp.where(left, float(TOK * 2 * m), float(TOK * (2 * m + 1)))
        where_ref[m : m + 1, :] = jnp.where((taken < 0.5) & (seen == 1), position, BIG)


def attend_kernel(far, q_ref, where_ref, start_ref, mine_ref, other_ref, *rest):
    scores = rest[-1]
    count = 2 * TOK
    is_key = lax.axis_index("head") % 2 == 0
    first = (lax.axis_index("seq") * TOK).astype(f32)
    slope = math.log2(math.e) / math.sqrt(HD)

    def tile_of(ref, t):
        if t < N_SEQ // 2:
            return ref[2 * t : 2 * t + 2, 0:HALF_TOK, :].reshape(HD, HD)
        m = t - N_SEQ // 2
        return ref[4 * m : 4 * m + 4, HALF_TOK : HALF_TOK + 32, :].reshape(HD, HD)

    def attend(keys, values):
        queries = q_ref[count:, :] if far else q_ref[:count, :]
        position = first + fiota((TOK, HD), 0)
        start = start_ref[...]
        top = jnp.full((count, HD), NEG, f32)
        for t in range(TILES):
            where = where_ref[t : t + 1, :]
            allowed = (where <= position) & (where >= start)
            allowed = jnp.concatenate([allowed] * 2, axis=0)
            score = jnp.where(allowed, dot_t(queries, tile_of(keys, t)), NEG)
            scores[t] = score
            top = jnp.maximum(top, score)
        top = jnp.maximum(jnp.max(top, axis=1, keepdims=True), LOW)
        total = jnp.zeros((count, HD), f32)
        mix = jnp.zeros((count, HD), f32)
        for t in range(TILES):
            weight = jnp.exp2((scores[t] - top) * slope)
            total = total + weight
            mix = mix + jnp.dot(weight.astype(bf16), tile_of(values, t), preferred_element_type=f32)
        total = jnp.sum(total, axis=1, keepdims=True)
        if not far:
            keep_ref = rest[0]
            keep_ref[0] = mix
            keep_ref[1] = jnp.broadcast_to(top, (count, HD))
            keep_ref[2] = jnp.broadcast_to(total, (count, HD))
            return
        send_ref = rest[0]
        send_ref[0:count, :] = (mix / jnp.maximum(total, 1.0e-30)).astype(bf16)
        rows = []
        for column in (top, total):
            for e in range(2):
                part = jnp.broadcast_to(column[e * TOK : (e + 1) * TOK], (TOK, HD))
                left = jnp.transpose(part)[0:1]
                for _ in range(3):
                    piece = left.astype(bf16).astype(f32)
                    rows.append(piece)
                    left = left - piece
        rows.append(jnp.zeros((4, HD), f32))
        send_ref[count:, :] = jnp.concatenate(rows, axis=0).astype(bf16)

    @pl.when(is_key)
    def _():
        attend(mine_ref, other_ref)

    @pl.when(jnp.logical_not(is_key))
    def _():
        attend(other_ref, mine_ref)


def combine_kernel(keep_ref, come_ref, out_ref):
    slope = math.log2(math.e) / math.sqrt(HD)
    pieces = come_ref[2 * TOK :, :].astype(f32)

    def column(i):
        row = pieces[3 * i : 3 * i + 1] + pieces[3 * i + 1 : 3 * i + 2] + pieces[3 * i + 2 : 3 * i + 3]
        return jnp.transpose(jnp.broadcast_to(row, (TOK, HD)))

    for e in range(2):
        span = slice(e * TOK, (e + 1) * TOK)
        top_near = keep_ref[1, span, :]
        top_far = column(e)
        top = jnp.maximum(top_near, top_far)
        near = jnp.exp2((top_near - top) * slope)
        far = jnp.exp2((top_far - top) * slope) * column(2 + e)
        mix = keep_ref[0, span, :] * near + come_ref[span, :].astype(f32) * far
        out_ref[:, e * HD : (e + 1) * HD] = (mix / (keep_ref[2, span, :] * near + far)).astype(bf16)


def vmem():
    return pl.BlockSpec(memory_space=pltpu.VMEM)


def small_params():
    return pltpu.CompilerParams(vmem_limit_bytes=SMALL)


def project_call(width):
    hbm = pl.BlockSpec(memory_space=pltpu.HBM)
    outputs = [
        ((N_HEAD, 8, HD), bf16),
        ((2 * TOK + N_SEQ * TAIL, HD), bf16),
        ((2 * KEYS + N_SEQ * TAIL, HD), f32),
        ((3 * TOK, HD), f32),
    ]
    call = pl.pallas_call(
        project_kernel,
        name="project",
        out_shape=tuple(jax.ShapeDtypeStruct(shape, dtype) for shape, dtype in outputs),
        in_specs=[hbm] * 11,
        out_specs=(vmem(),) * 4,
        scratch_shapes=[
            pltpu.VMEM((ROWS, width), bf16),
            pltpu.VMEM((width, 2 * HD), bf16),
            pltpu.VMEM((64, width), bf16),
            pltpu.VMEM((width,), bf16),
            pltpu.VMEM((2 * HD,), bf16),
            pltpu.VMEM((4, 8), bf16),
            pltpu.VMEM((1, IMG), jnp.int32),
            pltpu.VMEM((1, HD), f32),
            pltpu.SMEM((DOCS,), jnp.int32),
            pltpu.VMEM((2, ROWS, HD), f32),
            pltpu.SemaphoreType.DMA((4 + KCH,)),
            pltpu.SemaphoreType.DMA((6,)),
        ],
        compiler_params=pltpu.CompilerParams(vmem_limit_bytes=20 << 20),
    )
    return lambda *arrays: call(
        *(pltpu.with_memory_space_constraint(array, pltpu.HBM) for array in arrays)
    )


def attend_call(far):
    out = ((2 * TOK + 16, HD), bf16) if far else ((3, 2 * TOK, HD), f32)
    return pl.pallas_call(
        functools.partial(attend_kernel, far),
        name="attend_far" if far else "attend_near",
        out_shape=jax.ShapeDtypeStruct(*out),
        in_specs=[vmem()] * 5,
        out_specs=vmem(),
        scratch_shapes=[pltpu.VMEM((TILES, 2 * TOK, HD), f32)],
        compiler_params=small_params(),
        cost_estimate=pl.CostEstimate(flops=1 << 30, bytes_accessed=1 << 21, transcendentals=1 << 19),
    )


def panel_call():
    return pl.pallas_call(
        panel_kernel,
        name="panel",
        out_shape=jax.ShapeDtypeStruct((N_SEQ, PAY, HD), bf16),
        in_specs=[vmem()] * 3,
        out_specs=vmem(),
        compiler_params=small_params(),
    )


def body(
    embedded,
    norm_gain,
    query_weight,
    query_bias,
    key_weight,
    value_weight,
    value_bias,
    image_rows,
    image_dest,
    doc_lengths,
    block_mask,
):
    width = embedded.shape[1]
    half = np.arange(HD) % (HD // 2)
    inverse = jnp.asarray((rope_base ** (-2.0 * half / HD)).astype(np.float32)[None, :])
    smem = pl.BlockSpec(memory_space=pltpu.SMEM)
    key_t = jnp.transpose(key_weight, (1, 2, 0)).reshape(32, width)
    value_t = jnp.transpose(value_weight, (1, 2, 0)).reshape(32, width)
    kv_send, share, aux, own = project_call(width)(
        embedded, image_rows, query_weight, key_t, value_t, norm_gain, query_bias,
        value_bias, image_dest[None, :], inverse, doc_lengths,
    )
    chip_swap = [(i, i ^ 2) for i in range(N_HEAD)]
    core_swap = [(i, i ^ 1) for i in range(N_HEAD)]
    shared = lax.ppermute(share, "head", chip_swap)
    kv_mine = lax.all_to_all(kv_send, "head", 0, 0)
    payload = panel_call()(kv_mine, aux, shared)
    mine = lax.all_to_all(payload, "seq", 0, 0)
    other = lax.ppermute(mine, "head", core_swap)
    merged, where, start = pl.pallas_call(
        place_kernel,
        name="place",
        out_shape=(
            jax.ShapeDtypeStruct((4 * TOK, HD), bf16),
            jax.ShapeDtypeStruct((TILES, HD), f32),
            jax.ShapeDtypeStruct((TOK, HD), f32),
        ),
        in_specs=[vmem()] * 3 + [smem],
        out_specs=(vmem(),) * 3,
        compiler_params=small_params(),
        cost_estimate=pl.CostEstimate(flops=1 << 28, bytes_accessed=1 << 20, transcendentals=0),
    )(own, shared, mine, block_mask)
    send = attend_call(True)(merged, where, start, mine, other)
    come = lax.ppermute(send, "head", chip_swap)
    keep = attend_call(False)(merged, where, start, mine, other)
    return pl.pallas_call(
        combine_kernel,
        name="combine",
        out_shape=jax.ShapeDtypeStruct((TOK, 2 * HD), bf16),
        in_specs=[vmem()] * 2,
        out_specs=vmem(),
        compiler_params=small_params(),
    )(keep, come)


def solution(mesh):
    in_specs = (
        P("seq", None),
        P(),
        P(None, "head"),
        P("head"),
        P(None, None, "head"),
        P(None, None, "head"),
        P(None, "head"),
        P("seq", None),
        P("seq"),
        P(),
        P("seq", None),
    )
    out_specs = P("seq", "head")
    return jax.shard_map(body, mesh=mesh, in_specs=in_specs, out_specs=out_specs, check_vma=False)
```

```python
import functools
import math

import jax
import jax.numpy as jnp
import numpy as np
from jax import lax
from jax.experimental import pallas as pl
from jax.experimental.pallas import tpu as pltpu
from jax.sharding import PartitionSpec as P

HD = 128
GROUP = 8
BLK = 128
CAP = 6
TOK = 128
IMG = 48
N_SEQ = 16
N_HEAD = 16
ROWS = TOK + IMG
HALF_TOK = TOK // 2
HALF_IMG = IMG // 2
KEYS = HALF_TOK + HALF_IMG
TAIL = 16
PAY = KEYS + 2 * TAIL
PAIRS = N_SEQ // 2
TILES = PAIRS + N_SEQ // 4
MOST_DOC = 1152
REACH = MOST_DOC // TOK
WINDOW = REACH // 2 + 2
DOCS = 32
KCH = 4
LIMIT = 60 << 20
SMALL = 12 << 20

rope_base = 1000000.0
norm_eps = 1e-06
BIG = 1.0e6
NEG = -1.0e30
LOW = -1.0e29

f32 = jnp.float32
bf16 = jnp.bfloat16


def iota(shape, dim):
    return lax.broadcasted_iota(jnp.int32, shape, dim)


def fiota(shape, dim):
    return iota(shape, dim).astype(f32)


def dot_t(a, b):
    return lax.dot_general(a, b, (((1,), (1,)), ((), ())), preferred_element_type=f32)


def tdot(a, b):
    return lax.dot_general(a, b, (((0,), (0,)), ((), ())), preferred_element_type=f32)


def project_kernel(
    x_hbm, img_hbm, wq_hbm, wk_hbm, wv_hbm, gain_hbm, bq_hbm, bv_hbm, dest_hbm, invf_hbm, docs_hbm,
    kv_ref, share, aux, own,
    xs, wqs, wkvs, gains, bqs, bvs, dests, invfs, docs_ref, css, sems, small_sems,
):
    width = xs.shape[1]
    step = width // KCH
    copies = [
        pltpu.make_async_copy(x_hbm, xs.at[pl.ds(0, TOK)], sems.at[0]),
        pltpu.make_async_copy(img_hbm, xs.at[pl.ds(TOK, IMG)], sems.at[1]),
        pltpu.make_async_copy(wk_hbm, wkvs.at[pl.ds(0, 32)], sems.at[2]),
        pltpu.make_async_copy(wv_hbm, wkvs.at[pl.ds(32, 32)], sems.at[3]),
    ]
    for c in range(KCH):
        part = pl.ds(c * step, step)
        copies.append(pltpu.make_async_copy(wq_hbm.at[part], wqs.at[part], sems.at[4 + c]))
    small = [
        pltpu.make_async_copy(src, dst, small_sems.at[i])
        for i, (src, dst) in enumerate(
            ((docs_hbm, docs_ref), (dest_hbm, dests), (invf_hbm, invfs), (gain_hbm, gains), (bq_hbm, bqs), (bv_hbm, bvs))
        )
    ]
    for copy in small[:3] + copies[:2] + small[3:] + copies[2:]:
        copy.start()
    inverse = []
    for i, rows in enumerate((pl.ds(0, TOK), pl.ds(TOK, IMG))):
        copies[i].wait()
        squares = jnp.zeros((rows.size, HD), f32)
        for c in range(width // HD):
            wide = xs[rows, c * HD : (c + 1) * HD].astype(f32)
            squares = squares + wide * wide
        inverse.append(
            lax.rsqrt(jnp.sum(squares, axis=1, keepdims=True) * (1.0 / width) + norm_eps)
        )
    inverse = jnp.concatenate(inverse, axis=0)

    for copy in small[:3]:
        copy.wait()

    seq_place = lax.axis_index("seq")
    first = (seq_place * TOK).astype(f32)
    dest_row = dests[...].astype(f32)
    eye = iota((IMG, IMG), 0) == iota((IMG, IMG), 1)
    dest_col = jnp.sum(jnp.where(eye, dest_row, 0.0), axis=1, keepdims=True)
    hi_row = jnp.floor(dest_row * (1.0 / TOK))
    hi_col = jnp.floor(dest_col * (1.0 / TOK))
    lo_row = dest_row - TOK * hi_row
    lo_col = dest_col - TOK * hi_col

    index_col = jnp.concatenate([first + fiota((TOK, 1), 0), dest_col], axis=0)
    start_col = jnp.zeros((ROWS, 1), f32)
    begin = jnp.int32(0)
    for d in range(DOCS):
        begin_f = begin.astype(f32)
        start_col = jnp.where(index_col >= begin_f, begin_f, start_col)
        begin = begin + docs_ref[d]
    own[2 * TOK :, :] = jnp.broadcast_to(start_col[:TOK], (TOK, HD))
    angles = (index_col - start_col) * invfs[...]
    cosine = jnp.cos(angles)
    sine = jnp.sin(angles)
    sine = jnp.where(iota((ROWS, HD), 1) < HD // 2, -sine, sine)
    upper = (lax.axis_index("head") // 2) % 2 == 1
    for i, table in enumerate((cosine, sine)):
        css[i] = table
        low = i * KEYS
        aux[low : low + HALF_TOK, :] = jnp.where(upper, table[HALF_TOK:TOK], table[:HALF_TOK])
        aux[low + HALF_TOK : low + KEYS, :] = jnp.where(
            upper, table[TOK + HALF_IMG :], table[TOK : TOK + HALF_IMG]
        )

    for copy in small[3:] + copies[2:4]:
        copy.wait()
    queries = jnp.broadcast_to(bqs[...].astype(f32).reshape(1, 2 * HD), (ROWS, 2 * HD))
    kv = jnp.zeros((ROWS, 64), f32)
    for c in range(KCH):
        if c % 2 == 0:
            copies[4 + c].wait()
            copies[5 + c].wait()
        part = pl.ds(c * step, step)
        gain = gains[part].astype(f32).reshape(1, step)
        normed = (xs[:, part].astype(f32) * inverse * gain).astype(bf16)
        kv = kv + dot_t(normed, wkvs[:, part])
        queries = queries + jnp.dot(normed, wqs[part, :], preferred_element_type=f32)

    earlier = iota((IMG, IMG), 0) < iota((IMG, IMG), 1)
    later = iota((IMG, IMG), 0) > iota((IMG, IMG), 1)
    same = hi_col == hi_row
    rank_row = jnp.sum(jnp.where(same & earlier, 1.0, 0.0), axis=0, keepdims=True)
    rank_col = jnp.sum(jnp.where(same & later, 1.0, 0.0), axis=1, keepdims=True)
    count = N_SEQ * TAIL
    line = iota((count, IMG), 0)
    here = hi_row == (line // TAIL).astype(f32)
    slot = (line % TAIL).astype(f32)
    offsets = jnp.where(here & (slot == 14.0), lo_row + 1.0, 0.0).astype(bf16)
    lane = iota((IMG, HD), 1)
    ranked = jnp.where((rank_col == lane.astype(f32)) & (lane < CAP), 1.0, 0.0).astype(bf16)
    tail = jnp.dot(offsets, ranked, preferred_element_type=f32)
    skip = jnp.where(upper, HALF_IMG, 0)
    spread = (lane % 32 + skip == iota((IMG, HD), 0)) & (lane % 32 < HALF_IMG)
    unused = (iota((1, HD), 1) % 32) >= HALF_IMG
    hi_two = jnp.where(unused, 99.0, jnp.sum(jnp.where(spread, hi_col, 0.0), axis=0, keepdims=True))
    lo_two = jnp.sum(jnp.where(spread, lo_col, 0.0), axis=0, keepdims=True)
    wide_slot = iota((count, HD), 0) % TAIL
    tail = tail + jnp.where(wide_slot == 12, hi_two, jnp.where(wide_slot == 13, lo_two, 0.0))

    kv = jnp.concatenate([kv, jnp.zeros((ROWS, 64), f32)], axis=1)
    eye8 = iota((8, 8), 0) == iota((8, 8), 1)
    for j in range(2):
        kv_t = jnp.transpose(
            jnp.concatenate(
                [
                    kv[HALF_TOK * j : HALF_TOK * (j + 1)],
                    kv[TOK + HALF_IMG * j : TOK + HALF_IMG * (j + 1)],
                    jnp.zeros((HD - KEYS, HD), f32),
                ],
                axis=0,
            )
        )
        for g in range(4):
            bias_row = bvs[g : g + 1, :].astype(f32)
            bias = jnp.sum(jnp.where(eye8, bias_row, 0.0), axis=1, keepdims=True)
            kv_ref[4 * g + 2 * j] = kv_t[8 * g : 8 * g + 8].astype(bf16)
            kv_ref[4 * g + 2 * j + 1] = (kv_t[32 + 8 * g : 40 + 8 * g] + bias).astype(bf16)

    cosine = css[0]
    sine = css[1]
    for e in range(2):
        v = queries[:, e * HD : (e + 1) * HD]
        v = (v * cosine + pltpu.roll(v, HD // 2, 1) * sine).astype(bf16)
        share[e * TOK : (e + 1) * TOK, :] = v[:TOK]
        own[e * TOK : (e + 1) * TOK, :] = v[:TOK].astype(f32)
        pick = here & (rank_row == slot - CAP * e) & (slot >= CAP * e) & (slot < CAP * e + CAP)
        tail = tail + jnp.dot(
            jnp.where(pick, 1.0, 0.0).astype(bf16), v[TOK:], preferred_element_type=f32
        )
    share[2 * TOK :, :] = tail.astype(bf16)
    aux[2 * KEYS :, :] = tail


def panel_kernel(kv_ref, aux_ref, share_ref, pay_ref):
    is_key = lax.axis_index("head") % 2 == 0
    panel = jnp.transpose(kv_ref[...].astype(f32).reshape(HD, HD))[:KEYS]
    cosine = jnp.where(is_key, aux_ref[0:KEYS, :], 1.0)
    sine = jnp.where(is_key, aux_ref[KEYS : 2 * KEYS, :], 0.0)
    panel = (panel * cosine + pltpu.roll(panel, HD // 2, 1) * sine).astype(bf16)
    for p in range(N_SEQ):
        low = 2 * KEYS + TAIL * p
        pay_ref[p, 0:KEYS, :] = panel
        pay_ref[p, KEYS : KEYS + TAIL, :] = aux_ref[low : low + TAIL, :].astype(bf16)
        low = 2 * TOK + TAIL * p
        pay_ref[p, KEYS + TAIL : PAY, :] = share_ref[low : low + TAIL, :]


def place_kernel(own_ref, share_ref, mine_ref, mask_ref, merged_ref, where_ref, start_ref):
    start_ref[...] = own_ref[2 * TOK :, :]
    tails = mine_ref[:, KEYS:PAY, :].astype(f32)
    slots = tails[:, 14, :]
    count = N_SEQ * TAIL
    owner = iota((count, N_SEQ), 0) // TAIL == iota((count, N_SEQ), 1)
    spread = jnp.dot(
        jnp.where(owner, 1.0, 0.0).astype(bf16), slots.astype(bf16), preferred_element_type=f32
    )
    line = iota((count, HD), 0) % TAIL
    lane = iota((count, HD), 1)
    flats = [tails[:, c * TAIL : (c + 1) * TAIL, :].reshape(count, HD).astype(bf16) for c in range(2)]
    for e in range(2):
        slot = line - CAP * e
        used = (slot >= 0) & (slot < CAP)
        offset = jnp.sum(jnp.where(used & (lane == slot), spread, 0.0), axis=1, keepdims=True)
        place = jnp.where(offset == lane.astype(f32) + 1.0, 1.0, 0.0).astype(bf16)
        taken = tdot(place, jnp.ones((count, HD), bf16)) > 0.5
        span = slice(e * TOK, (e + 1) * TOK)
        merged_ref[span, :] = jnp.where(taken, tdot(place, flats[0]), own_ref[span, :]).astype(bf16)
        moved = jnp.where(taken, tdot(place, flats[1]), share_ref[span, :].astype(f32))
        merged_ref[(2 + e) * TOK : (3 + e) * TOK, :] = moved.astype(bf16)

    lane = iota((1, HD), 1)

    def four(rows, m):
        row = rows[4 * m + 3 : 4 * m + 4]
        for i in (2, 1, 0):
            row = jnp.where(lane < 32 * (i + 1), rows[4 * m + i : 4 * m + i + 1], row)
        return row

    covered = jnp.zeros((N_SEQ, HD), f32)
    for c in range(2):
        hi_all = tails[:, c * TAIL + 12, :]
        lo_all = tails[:, c * TAIL + 13, :]
        for m in range(N_SEQ // 4):
            hi = four(hi_all, m)
            lo = four(lo_all, m)
            hi_hot = jnp.where(hi == fiota((N_SEQ, HD), 0), 1.0, 0.0).astype(bf16)
            lo_hot = jnp.where(lo == fiota((HD, HD), 0), 1.0, 0.0).astype(bf16)
            covered = covered + dot_t(hi_hot, lo_hot)
            if c == 0:
                seen = jnp.zeros((1, HD), f32)
                for b in range(N_SEQ):
                    seen = jnp.where(hi == float(b), mask_ref[0, b].astype(f32), seen)
                at = N_SEQ // 2 + m
                where_ref[at : at + 1, :] = jnp.where(seen > 0.5, hi * float(TOK) + lo, BIG)
    upper = (lax.axis_index("head") // 2) % 2 == 1
    turned = pltpu.roll(covered, HALF_TOK, 1)
    near = jnp.where(upper, turned, covered)
    far = jnp.where(upper, covered, turned)
    base = (lane % HALF_TOK).astype(f32) + jnp.where(upper, float(HALF_TOK), 0.0)
    for m in range(N_SEQ // 2):
        left = lane < HALF_TOK
        taken = jnp.where(left, near[2 * m : 2 * m + 1], far[2 * m + 1 : 2 * m + 2])
        seen = jnp.where(left, mask_ref[0, 2 * m], mask_ref[0, 2 * m + 1])
        position = base + jnp.where(left, float(TOK * 2 * m), float(TOK * (2 * m + 1)))
        where_ref[m : m + 1, :] = jnp.where((taken < 0.5) & (seen == 1), position, BIG)


def attend_kernel(far, q_ref, where_ref, start_ref, mine_ref, other_ref, *rest):
    scores = rest[-1]
    count = 2 * TOK
    is_key = lax.axis_index("head") % 2 == 0
    first = (lax.axis_index("seq") * TOK).astype(f32)
    slope = math.log2(math.e) / math.sqrt(HD)

    low = jnp.maximum(lax.axis_index("seq") - REACH, 0) // 2
    low = jnp.minimum(low, PAIRS - WINDOW)

    def tile_of(ref, t):
        if t < WINDOW:
            return ref[pl.ds(2 * (low + t), 2), 0:HALF_TOK, :].reshape(HD, HD)
        m = t - WINDOW
        return ref[4 * m : 4 * m + 4, HALF_TOK : HALF_TOK + 32, :].reshape(HD, HD)

    def where_of(t):
        if t < WINDOW:
            return where_ref[pl.ds(low + t, 1), :]
        return where_ref[PAIRS + t - WINDOW : PAIRS + t - WINDOW + 1, :]

    steps = WINDOW + N_SEQ // 4

    def attend(keys, values):
        queries = q_ref[count:, :] if far else q_ref[:count, :]
        position = first + fiota((TOK, HD), 0)
        start = start_ref[...]
        top = jnp.full((count, HD), NEG, f32)
        for t in range(steps):
            where = where_of(t)
            allowed = (where <= position) & (where >= start)
            allowed = jnp.concatenate([allowed] * 2, axis=0)
            score = jnp.where(allowed, dot_t(queries, tile_of(keys, t)), NEG)
            scores[t] = score
            top = jnp.maximum(top, score)
        top = jnp.maximum(jnp.max(top, axis=1, keepdims=True), LOW)
        total = jnp.zeros((count, HD), f32)
        mix = jnp.zeros((count, HD), f32)
        for t in range(steps):
            weight = jnp.exp2((scores[t] - top) * slope)
            total = total + weight
            mix = mix + jnp.dot(weight.astype(bf16), tile_of(values, t), preferred_element_type=f32)
        total = jnp.sum(total, axis=1, keepdims=True)
        if not far:
            keep_ref = rest[0]
            keep_ref[0] = mix
            keep_ref[1] = jnp.broadcast_to(top, (count, HD))
            keep_ref[2] = jnp.broadcast_to(total, (count, HD))
            return
        send_ref = rest[0]
        send_ref[0:count, :] = (mix / jnp.maximum(total, 1.0e-30)).astype(bf16)
        rows = []
        for column in (top, total):
            for e in range(2):
                part = jnp.broadcast_to(column[e * TOK : (e + 1) * TOK], (TOK, HD))
                left = jnp.transpose(part)[0:1]
                for _ in range(3):
                    piece = left.astype(bf16).astype(f32)
                    rows.append(piece)
                    left = left - piece
        rows.append(jnp.zeros((4, HD), f32))
        send_ref[count:, :] = jnp.concatenate(rows, axis=0).astype(bf16)

    @pl.when(is_key)
    def _():
        attend(mine_ref, other_ref)

    @pl.when(jnp.logical_not(is_key))
    def _():
        attend(other_ref, mine_ref)


def combine_kernel(keep_ref, come_ref, out_ref):
    slope = math.log2(math.e) / math.sqrt(HD)
    pieces = come_ref[2 * TOK :, :].astype(f32)

    def column(i):
        row = pieces[3 * i : 3 * i + 1] + pieces[3 * i + 1 : 3 * i + 2] + pieces[3 * i + 2 : 3 * i + 3]
        return jnp.transpose(jnp.broadcast_to(row, (TOK, HD)))

    for e in range(2):
        span = slice(e * TOK, (e + 1) * TOK)
        top_near = keep_ref[1, span, :]
        top_far = column(e)
        top = jnp.maximum(top_near, top_far)
        near = jnp.exp2((top_near - top) * slope)
        far = jnp.exp2((top_far - top) * slope) * column(2 + e)
        mix = keep_ref[0, span, :] * near + come_ref[span, :].astype(f32) * far
        out_ref[:, e * HD : (e + 1) * HD] = (mix / (keep_ref[2, span, :] * near + far)).astype(bf16)


def vmem():
    return pl.BlockSpec(memory_space=pltpu.VMEM)


def small_params():
    return pltpu.CompilerParams(vmem_limit_bytes=SMALL)


def project_call(width):
    hbm = pl.BlockSpec(memory_space=pltpu.HBM)
    outputs = [
        ((N_HEAD, 8, HD), bf16),
        ((2 * TOK + N_SEQ * TAIL, HD), bf16),
        ((2 * KEYS + N_SEQ * TAIL, HD), f32),
        ((3 * TOK, HD), f32),
    ]
    call = pl.pallas_call(
        project_kernel,
        name="project",
        out_shape=tuple(jax.ShapeDtypeStruct(shape, dtype) for shape, dtype in outputs),
        in_specs=[hbm] * 11,
        out_specs=(vmem(),) * 4,
        scratch_shapes=[
            pltpu.VMEM((ROWS, width), bf16),
            pltpu.VMEM((width, 2 * HD), bf16),
            pltpu.VMEM((64, width), bf16),
            pltpu.VMEM((width,), bf16),
            pltpu.VMEM((2 * HD,), bf16),
            pltpu.VMEM((4, 8), bf16),
            pltpu.VMEM((1, IMG), jnp.int32),
            pltpu.VMEM((1, HD), f32),
            pltpu.SMEM((DOCS,), jnp.int32),
            pltpu.VMEM((2, ROWS, HD), f32),
            pltpu.SemaphoreType.DMA((4 + KCH,)),
            pltpu.SemaphoreType.DMA((6,)),
        ],
        compiler_params=pltpu.CompilerParams(vmem_limit_bytes=20 << 20),
    )
    return lambda *arrays: call(
        *(pltpu.with_memory_space_constraint(array, pltpu.HBM) for array in arrays)
    )


def attend_call(far):
    out = ((2 * TOK + 16, HD), bf16) if far else ((3, 2 * TOK, HD), f32)
    return pl.pallas_call(
        functools.partial(attend_kernel, far),
        name="attend_far" if far else "attend_near",
        out_shape=jax.ShapeDtypeStruct(*out),
        in_specs=[vmem()] * 5,
        out_specs=vmem(),
        scratch_shapes=[pltpu.VMEM((WINDOW + N_SEQ // 4, 2 * TOK, HD), f32)],
        compiler_params=small_params(),
        cost_estimate=pl.CostEstimate(flops=1 << 30, bytes_accessed=1 << 21, transcendentals=1 << 19),
    )


def panel_call():
    return pl.pallas_call(
        panel_kernel,
        name="panel",
        out_shape=jax.ShapeDtypeStruct((N_SEQ, PAY, HD), bf16),
        in_specs=[vmem()] * 3,
        out_specs=vmem(),
        compiler_params=small_params(),
    )


def body(
    embedded,
    norm_gain,
    query_weight,
    query_bias,
    key_weight,
    value_weight,
    value_bias,
    image_rows,
    image_dest,
    doc_lengths,
    block_mask,
):
    width = embedded.shape[1]
    half = np.arange(HD) % (HD // 2)
    inverse = jnp.asarray((rope_base ** (-2.0 * half / HD)).astype(np.float32)[None, :])
    smem = pl.BlockSpec(memory_space=pltpu.SMEM)
    key_t = jnp.transpose(key_weight, (1, 2, 0)).reshape(32, width)
    value_t = jnp.transpose(value_weight, (1, 2, 0)).reshape(32, width)
    kv_send, share, aux, own = project_call(width)(
        embedded, image_rows, query_weight, key_t, value_t, norm_gain, query_bias,
        value_bias, image_dest[None, :], inverse, doc_lengths,
    )
    chip_swap = [(i, i ^ 2) for i in range(N_HEAD)]
    core_swap = [(i, i ^ 1) for i in range(N_HEAD)]
    shared = lax.ppermute(share, "head", chip_swap)
    kv_mine = lax.all_to_all(kv_send, "head", 0, 0)
    payload = panel_call()(kv_mine, aux, shared)
    mine = lax.all_to_all(payload, "seq", 0, 0)
    other = lax.ppermute(mine, "head", core_swap)
    merged, where, start = pl.pallas_call(
        place_kernel,
        name="place",
        out_shape=(
            jax.ShapeDtypeStruct((4 * TOK, HD), bf16),
            jax.ShapeDtypeStruct((TILES, HD), f32),
            jax.ShapeDtypeStruct((TOK, HD), f32),
        ),
        in_specs=[vmem()] * 3 + [smem],
        out_specs=(vmem(),) * 3,
        compiler_params=small_params(),
        cost_estimate=pl.CostEstimate(flops=1 << 28, bytes_accessed=1 << 20, transcendentals=0),
    )(own, shared, mine, block_mask)
    send = attend_call(True)(merged, where, start, mine, other)
    come = lax.ppermute(send, "head", chip_swap)
    keep = attend_call(False)(merged, where, start, mine, other)
    return pl.pallas_call(
        combine_kernel,
        name="combine",
        out_shape=jax.ShapeDtypeStruct((TOK, 2 * HD), bf16),
        in_specs=[vmem()] * 2,
        out_specs=vmem(),
        compiler_params=small_params(),
    )(keep, come)


def solution(mesh):
    in_specs = (
        P("seq", None),
        P(),
        P(None, "head"),
        P("head"),
        P(None, None, "head"),
        P(None, None, "head"),
        P(None, "head"),
        P("seq", None),
        P("seq"),
        P(),
        P("seq", None),
    )
    out_specs = P("seq", "head")
    return jax.shard_map(body, mesh=mesh, in_specs=in_specs, out_specs=out_specs, check_vma=False)
```

```python
import functools
import math

import jax
import jax.numpy as jnp
import numpy as np
from jax import lax
from jax.experimental import pallas as pl
from jax.experimental.pallas import tpu as pltpu
from jax.sharding import PartitionSpec as P

HD = 128
GROUP = 8
BLK = 128
CAP = 6
TOK = 128
IMG = 48
N_SEQ = 16
N_HEAD = 16
ROWS = TOK + IMG
HALF_TOK = TOK // 2
HALF_IMG = IMG // 2
KEYS = HALF_TOK + HALF_IMG
TAIL = 16
PAY = KEYS + 2 * TAIL
PAIRS = N_SEQ // 2
MOST_DOC = 1152
REACH = MOST_DOC // TOK
WINDOW = REACH // 2 + 2
DOCS = 32
KCH = 4
LIMIT = 60 << 20
SMALL = 12 << 20

rope_base = 1000000.0
norm_eps = 1e-06
BIG = 1.0e6
NEG = -1.0e30
LOW = -1.0e29

f32 = jnp.float32
bf16 = jnp.bfloat16


def iota(shape, dim):
    return lax.broadcasted_iota(jnp.int32, shape, dim)


def fiota(shape, dim):
    return iota(shape, dim).astype(f32)


def dot_t(a, b):
    return lax.dot_general(a, b, (((1,), (1,)), ((), ())), preferred_element_type=f32)


def tdot(a, b):
    return lax.dot_general(a, b, (((0,), (0,)), ((), ())), preferred_element_type=f32)


def project_kernel(
    x_hbm, img_hbm, wq_hbm, wk_hbm, wv_hbm, gain_hbm, bq_hbm, bv_hbm, dest_hbm, invf_hbm, docs_hbm,
    kv_ref, share, aux, own,
    xs, wqs, wkvs, gains, bqs, bvs, dests, invfs, docs_ref, css, sems, small_sems,
):
    width = xs.shape[1]
    step = width // KCH
    copies = [
        pltpu.make_async_copy(x_hbm, xs.at[pl.ds(0, TOK)], sems.at[0]),
        pltpu.make_async_copy(img_hbm, xs.at[pl.ds(TOK, IMG)], sems.at[1]),
        pltpu.make_async_copy(wk_hbm, wkvs.at[pl.ds(0, 32)], sems.at[2]),
        pltpu.make_async_copy(wv_hbm, wkvs.at[pl.ds(32, 32)], sems.at[3]),
    ]
    for c in range(KCH):
        part = pl.ds(c * step, step)
        copies.append(pltpu.make_async_copy(wq_hbm.at[part], wqs.at[part], sems.at[4 + c]))
    small = [
        pltpu.make_async_copy(src, dst, small_sems.at[i])
        for i, (src, dst) in enumerate(
            ((docs_hbm, docs_ref), (dest_hbm, dests), (invf_hbm, invfs), (gain_hbm, gains), (bq_hbm, bqs), (bv_hbm, bvs))
        )
    ]
    for copy in small[:3] + copies[:2] + small[3:] + copies[2:]:
        copy.start()
    inverse = []
    for i, rows in enumerate((pl.ds(0, TOK), pl.ds(TOK, IMG))):
        copies[i].wait()
        squares = jnp.zeros((rows.size, HD), f32)
        for c in range(width // HD):
            wide = xs[rows, c * HD : (c + 1) * HD].astype(f32)
            squares = squares + wide * wide
        inverse.append(
            lax.rsqrt(jnp.sum(squares, axis=1, keepdims=True) * (1.0 / width) + norm_eps)
        )
    inverse = jnp.concatenate(inverse, axis=0)

    for copy in small[:3]:
        copy.wait()

    seq_place = lax.axis_index("seq")
    first = (seq_place * TOK).astype(f32)
    dest_row = dests[...].astype(f32)
    eye = iota((IMG, IMG), 0) == iota((IMG, IMG), 1)
    dest_col = jnp.sum(jnp.where(eye, dest_row, 0.0), axis=1, keepdims=True)
    hi_row = jnp.floor(dest_row * (1.0 / TOK))
    hi_col = jnp.floor(dest_col * (1.0 / TOK))
    lo_row = dest_row - TOK * hi_row
    lo_col = dest_col - TOK * hi_col

    token_row = first + fiota((1, TOK), 1)
    token_start = jnp.zeros((1, TOK), f32)
    image_start = jnp.zeros((1, IMG), f32)
    begin = jnp.int32(0)
    for d in range(DOCS):
        begin_f = begin.astype(f32)
        token_start = jnp.where(token_row >= begin_f, begin_f, token_start)
        image_start = jnp.where(dest_row >= begin_f, begin_f, image_start)
        begin = begin + docs_ref[d]
    image_start = jnp.sum(jnp.where(eye, image_start, 0.0), axis=1, keepdims=True)
    token_start = jnp.transpose(jnp.broadcast_to(token_start, (TOK, TOK)))
    index_col = jnp.concatenate([first + fiota((TOK, HD), 0), jnp.broadcast_to(dest_col, (IMG, HD))], axis=0)
    start_col = jnp.concatenate([token_start, jnp.broadcast_to(image_start, (IMG, HD))], axis=0)
    own[2 * TOK :, :] = start_col[:TOK]
    angles = (index_col - start_col) * invfs[...]
    cosine = jnp.cos(angles)
    sine = jnp.sin(angles)
    sine = jnp.where(iota((ROWS, HD), 1) < HD // 2, -sine, sine)
    upper = (lax.axis_index("head") // 2) % 2 == 1
    for i, table in enumerate((cosine, sine)):
        css[i] = table
        low = i * KEYS
        aux[low : low + HALF_TOK, :] = jnp.where(upper, table[HALF_TOK:TOK], table[:HALF_TOK])
        aux[low + HALF_TOK : low + KEYS, :] = jnp.where(
            upper, table[TOK + HALF_IMG :], table[TOK : TOK + HALF_IMG]
        )

    for copy in small[3:] + copies[2:4]:
        copy.wait()
    queries = jnp.broadcast_to(bqs[...].astype(f32).reshape(1, 2 * HD), (ROWS, 2 * HD))
    kv = jnp.zeros((ROWS, 64), f32)
    for c in range(KCH):
        if c % 2 == 0:
            copies[4 + c].wait()
            copies[5 + c].wait()
        part = pl.ds(c * step, step)
        gain = gains[part].astype(f32).reshape(1, step)
        normed = (xs[:, part].astype(f32) * inverse * gain).astype(bf16)
        kv = kv + dot_t(normed, wkvs[:, part])
        queries = queries + jnp.dot(normed, wqs[part, :], preferred_element_type=f32)

    earlier = iota((IMG, IMG), 0) < iota((IMG, IMG), 1)
    later = iota((IMG, IMG), 0) > iota((IMG, IMG), 1)
    same = hi_col == hi_row
    rank_row = jnp.sum(jnp.where(same & earlier, 1.0, 0.0), axis=0, keepdims=True)
    rank_col = jnp.sum(jnp.where(same & later, 1.0, 0.0), axis=1, keepdims=True)
    count = N_SEQ * TAIL
    line = iota((count, IMG), 0)
    here = hi_row == (line // TAIL).astype(f32)
    slot = (line % TAIL).astype(f32)
    offsets = jnp.where(here & (slot == 14.0), lo_row + 1.0, 0.0).astype(bf16)
    lane = iota((IMG, HD), 1)
    ranked = jnp.where((rank_col == lane.astype(f32)) & (lane < CAP), 1.0, 0.0).astype(bf16)
    tail = jnp.dot(offsets, ranked, preferred_element_type=f32)
    skip = jnp.where(upper, HALF_IMG, 0)
    spread = (lane % 32 + skip == iota((IMG, HD), 0)) & (lane % 32 < HALF_IMG)
    unused = (iota((1, HD), 1) % 32) >= HALF_IMG
    hi_two = jnp.where(unused, 99.0, jnp.sum(jnp.where(spread, hi_col, 0.0), axis=0, keepdims=True))
    lo_two = jnp.sum(jnp.where(spread, lo_col, 0.0), axis=0, keepdims=True)
    wide_slot = iota((count, HD), 0) % TAIL
    tail = tail + jnp.where(wide_slot == 12, hi_two, jnp.where(wide_slot == 13, lo_two, 0.0))

    kv = jnp.concatenate([kv, jnp.zeros((ROWS, 64), f32)], axis=1)
    eye8 = iota((8, 8), 0) == iota((8, 8), 1)
    for j in range(2):
        kv_t = jnp.transpose(
            jnp.concatenate(
                [
                    kv[HALF_TOK * j : HALF_TOK * (j + 1)],
                    kv[TOK + HALF_IMG * j : TOK + HALF_IMG * (j + 1)],
                    jnp.zeros((HD - KEYS, HD), f32),
                ],
                axis=0,
            )
        )
        for g in range(4):
            bias_row = bvs[g : g + 1, :].astype(f32)
            bias = jnp.sum(jnp.where(eye8, bias_row, 0.0), axis=1, keepdims=True)
            kv_ref[4 * g + 2 * j] = kv_t[8 * g : 8 * g + 8].astype(bf16)
            kv_ref[4 * g + 2 * j + 1] = (kv_t[32 + 8 * g : 40 + 8 * g] + bias).astype(bf16)

    cosine = css[0]
    sine = css[1]
    for e in range(2):
        v = queries[:, e * HD : (e + 1) * HD]
        v = (v * cosine + pltpu.roll(v, HD // 2, 1) * sine).astype(bf16)
        share[e * TOK : (e + 1) * TOK, :] = v[:TOK]
        own[e * TOK : (e + 1) * TOK, :] = v[:TOK].astype(f32)
        pick = here & (rank_row == slot - CAP * e) & (slot >= CAP * e) & (slot < CAP * e + CAP)
        tail = tail + jnp.dot(
            jnp.where(pick, 1.0, 0.0).astype(bf16), v[TOK:], preferred_element_type=f32
        )
    share[2 * TOK :, :] = tail.astype(bf16)
    aux[2 * KEYS :, :] = tail


def panel_kernel(kv_ref, aux_ref, share_ref, pay_ref):
    is_key = lax.axis_index("head") % 2 == 0
    panel = jnp.transpose(kv_ref[...].astype(f32).reshape(HD, HD))[:KEYS]
    cosine = jnp.where(is_key, aux_ref[0:KEYS, :], 1.0)
    sine = jnp.where(is_key, aux_ref[KEYS : 2 * KEYS, :], 0.0)
    panel = (panel * cosine + pltpu.roll(panel, HD // 2, 1) * sine).astype(bf16)
    for p in range(N_SEQ):
        low = 2 * KEYS + TAIL * p
        pay_ref[p, 0:KEYS, :] = panel
        pay_ref[p, KEYS : KEYS + TAIL, :] = aux_ref[low : low + TAIL, :].astype(bf16)
        low = 2 * TOK + TAIL * p
        pay_ref[p, KEYS + TAIL : PAY, :] = share_ref[low : low + TAIL, :]


def place_kernel(own_ref, share_ref, mine_ref, mask_ref, merged_ref, where_ref, start_ref):
    start_ref[...] = own_ref[2 * TOK :, :]
    tails = mine_ref[:, KEYS:PAY, :].astype(f32)
    slots = tails[:, 14, :]
    count = N_SEQ * TAIL
    owner = iota((count, N_SEQ), 0) // TAIL == iota((count, N_SEQ), 1)
    spread = jnp.dot(
        jnp.where(owner, 1.0, 0.0).astype(bf16), slots.astype(bf16), preferred_element_type=f32
    )
    line = iota((count, HD), 0) % TAIL
    lane = iota((count, HD), 1)
    flats = [tails[:, c * TAIL : (c + 1) * TAIL, :].reshape(count, HD).astype(bf16) for c in range(2)]
    for e in range(2):
        slot = line - CAP * e
        used = (slot >= 0) & (slot < CAP)
        offset = jnp.sum(jnp.where(used & (lane == slot), spread, 0.0), axis=1, keepdims=True)
        place = jnp.where(offset == lane.astype(f32) + 1.0, 1.0, 0.0).astype(bf16)
        taken = tdot(place, jnp.ones((count, HD), bf16)) > 0.5
        span = slice(e * TOK, (e + 1) * TOK)
        merged_ref[span, :] = jnp.where(taken, tdot(place, flats[0]), own_ref[span, :]).astype(bf16)
        moved = jnp.where(taken, tdot(place, flats[1]), share_ref[span, :].astype(f32))
        merged_ref[(2 + e) * TOK : (3 + e) * TOK, :] = moved.astype(bf16)

    lane = iota((1, HD), 1)

    def four(rows, m):
        row = rows[4 * m + 3 : 4 * m + 4]
        for i in (2, 1, 0):
            row = jnp.where(lane < 32 * (i + 1), rows[4 * m + i : 4 * m + i + 1], row)
        return row

    covered = jnp.zeros((N_SEQ, HD), f32)
    for c in range(2):
        hi_all = tails[:, c * TAIL + 12, :]
        lo_all = tails[:, c * TAIL + 13, :]
        for m in range(N_SEQ // 4):
            hi = four(hi_all, m)
            lo = four(lo_all, m)
            hi_hot = jnp.where(hi == fiota((N_SEQ, HD), 0), 1.0, 0.0).astype(bf16)
            lo_hot = jnp.where(lo == fiota((HD, HD), 0), 1.0, 0.0).astype(bf16)
            covered = covered + dot_t(hi_hot, lo_hot)
            if c == 0:
                seen = jnp.zeros((1, HD), f32)
                for b in range(N_SEQ):
                    seen = jnp.where(hi == float(b), mask_ref[0, b].astype(f32), seen)
                at = N_SEQ // 2 + m
                where_ref[at : at + 1, :] = jnp.where(seen > 0.5, hi * float(TOK) + lo, BIG)
    upper = (lax.axis_index("head") // 2) % 2 == 1
    turned = pltpu.roll(covered, HALF_TOK, 1)
    near = jnp.where(upper, turned, covered)
    far = jnp.where(upper, covered, turned)
    base = (lane % HALF_TOK).astype(f32) + jnp.where(upper, float(HALF_TOK), 0.0)
    for m in range(N_SEQ // 2):
        left = lane < HALF_TOK
        taken = jnp.where(left, near[2 * m : 2 * m + 1], far[2 * m + 1 : 2 * m + 2])
        seen = jnp.where(left, mask_ref[0, 2 * m], mask_ref[0, 2 * m + 1])
        position = base + jnp.where(left, float(TOK * 2 * m), float(TOK * (2 * m + 1)))
        where_ref[m : m + 1, :] = jnp.where((taken < 0.5) & (seen == 1), position, BIG)


def attend_kernel(far, q_ref, where_ref, start_ref, mine_ref, other_ref, *rest):
    scores = rest[-1]
    count = 2 * TOK
    is_key = lax.axis_index("head") % 2 == 0
    first = (lax.axis_index("seq") * TOK).astype(f32)
    slope = math.log2(math.e) / math.sqrt(HD)

    low = jnp.maximum(lax.axis_index("seq") - REACH, 0) // 2
    low = jnp.minimum(low, PAIRS - WINDOW)

    def tile_of(ref, t):
        if t < WINDOW:
            return ref[pl.ds(2 * (low + t), 2), 0:HALF_TOK, :].reshape(HD, HD)
        m = t - WINDOW
        return ref[4 * m : 4 * m + 4, HALF_TOK : HALF_TOK + 32, :].reshape(HD, HD)

    def where_of(t):
        if t < WINDOW:
            return where_ref[pl.ds(low + t, 1), :]
        return where_ref[PAIRS + t - WINDOW : PAIRS + t - WINDOW + 1, :]

    steps = WINDOW + N_SEQ // 4

    def attend(keys, values):
        queries = q_ref[count:, :] if far else q_ref[:count, :]
        position = first + fiota((TOK, HD), 0)
        start = start_ref[...]
        top = jnp.full((count, HD), NEG, f32)
        for t in range(steps):
            where = where_of(t)
            allowed = (where <= position) & (where >= start)
            allowed = jnp.concatenate([allowed] * 2, axis=0)
            score = jnp.where(allowed, dot_t(queries, tile_of(keys, t)), NEG)
            scores[t] = score
            top = jnp.maximum(top, score)
        top = jnp.maximum(jnp.max(top, axis=1, keepdims=True), LOW)
        total = jnp.zeros((count, HD), f32)
        mix = jnp.zeros((count, HD), f32)
        for t in range(steps):
            weight = jnp.exp2((scores[t] - top) * slope)
            total = total + weight
            mix = mix + jnp.dot(weight.astype(bf16), tile_of(values, t), preferred_element_type=f32)
        total = jnp.sum(total, axis=1, keepdims=True)
        if not far:
            keep_ref = rest[0]
            keep_ref[0] = mix
            keep_ref[1] = jnp.broadcast_to(top, (count, HD))
            keep_ref[2] = jnp.broadcast_to(total, (count, HD))
            return
        send_ref = rest[0]
        send_ref[0:count, :] = (mix / jnp.maximum(total, 1.0e-30)).astype(bf16)
        rows = []
        for column in (top, total):
            for e in range(2):
                part = jnp.broadcast_to(column[e * TOK : (e + 1) * TOK], (TOK, HD))
                left = jnp.transpose(part)[0:1]
                for _ in range(3):
                    piece = left.astype(bf16).astype(f32)
                    rows.append(piece)
                    left = left - piece
        rows.append(jnp.zeros((4, HD), f32))
        send_ref[count:, :] = jnp.concatenate(rows, axis=0).astype(bf16)

    @pl.when(is_key)
    def _():
        attend(mine_ref, other_ref)

    @pl.when(jnp.logical_not(is_key))
    def _():
        attend(other_ref, mine_ref)


def combine_kernel(keep_ref, come_ref, out_ref):
    slope = math.log2(math.e) / math.sqrt(HD)
    pieces = come_ref[2 * TOK :, :].astype(f32)

    def column(i):
        row = pieces[3 * i : 3 * i + 1] + pieces[3 * i + 1 : 3 * i + 2] + pieces[3 * i + 2 : 3 * i + 3]
        return jnp.transpose(jnp.broadcast_to(row, (TOK, HD)))

    for e in range(2):
        span = slice(e * TOK, (e + 1) * TOK)
        top_near = keep_ref[1, span, :]
        top_far = column(e)
        top = jnp.maximum(top_near, top_far)
        near = jnp.exp2((top_near - top) * slope)
        far = jnp.exp2((top_far - top) * slope) * column(2 + e)
        mix = keep_ref[0, span, :] * near + come_ref[span, :].astype(f32) * far
        out_ref[:, e * HD : (e + 1) * HD] = (mix / (keep_ref[2, span, :] * near + far)).astype(bf16)


def vmem():
    return pl.BlockSpec(memory_space=pltpu.VMEM)


def small_params():
    return pltpu.CompilerParams(vmem_limit_bytes=SMALL)


def project_call(width):
    hbm = pl.BlockSpec(memory_space=pltpu.HBM)
    outputs = [
        ((N_HEAD, 8, HD), bf16),
        ((2 * TOK + N_SEQ * TAIL, HD), bf16),
        ((2 * KEYS + N_SEQ * TAIL, HD), f32),
        ((3 * TOK, HD), f32),
    ]
    call = pl.pallas_call(
        project_kernel,
        name="project",
        out_shape=tuple(jax.ShapeDtypeStruct(shape, dtype) for shape, dtype in outputs),
        in_specs=[hbm] * 11,
        out_specs=(vmem(),) * 4,
        scratch_shapes=[
            pltpu.VMEM((ROWS, width), bf16),
            pltpu.VMEM((width, 2 * HD), bf16),
            pltpu.VMEM((64, width), bf16),
            pltpu.VMEM((width,), bf16),
            pltpu.VMEM((2 * HD,), bf16),
            pltpu.VMEM((4, 8), bf16),
            pltpu.VMEM((1, IMG), jnp.int32),
            pltpu.VMEM((1, HD), f32),
            pltpu.SMEM((DOCS,), jnp.int32),
            pltpu.VMEM((2, ROWS, HD), f32),
            pltpu.SemaphoreType.DMA((4 + KCH,)),
            pltpu.SemaphoreType.DMA((6,)),
        ],
        compiler_params=pltpu.CompilerParams(vmem_limit_bytes=20 << 20),
    )
    return lambda *arrays: call(
        *(pltpu.with_memory_space_constraint(array, pltpu.HBM) for array in arrays)
    )


def attend_call(far):
    out = ((2 * TOK + 16, HD), bf16) if far else ((3, 2 * TOK, HD), f32)
    return pl.pallas_call(
        functools.partial(attend_kernel, far),
        name="attend_far" if far else "attend_near",
        out_shape=jax.ShapeDtypeStruct(*out),
        in_specs=[vmem()] * 5,
        out_specs=vmem(),
        scratch_shapes=[pltpu.VMEM((WINDOW + N_SEQ // 4, 2 * TOK, HD), f32)],
        compiler_params=small_params(),
        cost_estimate=pl.CostEstimate(flops=1 << 30, bytes_accessed=1 << 21, transcendentals=1 << 19),
    )


def panel_call():
    return pl.pallas_call(
        panel_kernel,
        name="panel",
        out_shape=jax.ShapeDtypeStruct((N_SEQ, PAY, HD), bf16),
        in_specs=[vmem()] * 3,
        out_specs=vmem(),
        compiler_params=small_params(),
    )


def body(
    embedded,
    norm_gain,
    query_weight,
    query_bias,
    key_weight,
    value_weight,
    value_bias,
    image_rows,
    image_dest,
    doc_lengths,
    block_mask,
):
    width = embedded.shape[1]
    half = np.arange(HD) % (HD // 2)
    inverse = jnp.asarray((rope_base ** (-2.0 * half / HD)).astype(np.float32)[None, :])
    smem = pl.BlockSpec(memory_space=pltpu.SMEM)
    key_t = jnp.transpose(key_weight, (1, 2, 0)).reshape(32, width)
    value_t = jnp.transpose(value_weight, (1, 2, 0)).reshape(32, width)
    kv_send, share, aux, own = project_call(width)(
        embedded, image_rows, query_weight, key_t, value_t, norm_gain, query_bias,
        value_bias, image_dest[None, :], inverse, doc_lengths,
    )
    chip_swap = [(i, i ^ 2) for i in range(N_HEAD)]
    core_swap = [(i, i ^ 1) for i in range(N_HEAD)]
    shared = lax.ppermute(share, "head", chip_swap)
    kv_mine = lax.all_to_all(kv_send, "head", 0, 0)
    payload = panel_call()(kv_mine, aux, shared)
    mine = lax.all_to_all(payload, "seq", 0, 0)
    other = lax.ppermute(mine, "head", core_swap)
    merged, where, start = pl.pallas_call(
        place_kernel,
        name="place",
        out_shape=(
            jax.ShapeDtypeStruct((4 * TOK, HD), bf16),
            jax.ShapeDtypeStruct((N_SEQ, HD), f32),
            jax.ShapeDtypeStruct((TOK, HD), f32),
        ),
        in_specs=[vmem()] * 3 + [smem],
        out_specs=(vmem(),) * 3,
        compiler_params=small_params(),
        cost_estimate=pl.CostEstimate(flops=1 << 28, bytes_accessed=1 << 20, transcendentals=0),
    )(own, shared, mine, block_mask)
    send = attend_call(True)(merged, where, start, mine, other)
    come = lax.ppermute(send, "head", chip_swap)
    keep = attend_call(False)(merged, where, start, mine, other)
    return pl.pallas_call(
        combine_kernel,
        name="combine",
        out_shape=jax.ShapeDtypeStruct((TOK, 2 * HD), bf16),
        in_specs=[vmem()] * 2,
        out_specs=vmem(),
        compiler_params=small_params(),
    )(keep, come)


def solution(mesh):
    in_specs = (
        P("seq", None),
        P(),
        P(None, "head"),
        P("head"),
        P(None, None, "head"),
        P(None, None, "head"),
        P(None, "head"),
        P("seq", None),
        P("seq"),
        P(),
        P("seq", None),
    )
    out_specs = P("seq", "head")
    return jax.shard_map(body, mesh=mesh, in_specs=in_specs, out_specs=out_specs, check_vma=False)
```

```python
import functools
import math

import jax
import jax.numpy as jnp
import numpy as np
from jax import lax
from jax.experimental import pallas as pl
from jax.experimental.pallas import tpu as pltpu
from jax.sharding import PartitionSpec as P

HD = 128
GROUP = 8
BLK = 128
CAP = 6
TOK = 128
IMG = 48
N_SEQ = 16
N_HEAD = 16
ROWS = TOK + IMG
HALF_TOK = TOK // 2
HALF_IMG = IMG // 2
KEYS = HALF_TOK + HALF_IMG
TAIL = 16
PAY = KEYS + 2 * TAIL
PAIRS = N_SEQ // 2
TILES = PAIRS + N_SEQ // 4
MOST_DOC = 1152
REACH = MOST_DOC // TOK
WINDOW = REACH // 2 + 2
DOCS = 32
KCH = 4
LIMIT = 60 << 20
SMALL = 12 << 20

rope_base = 1000000.0
norm_eps = 1e-06
BIG = 1.0e6
NEG = -1.0e30
LOW = -1.0e29

f32 = jnp.float32
bf16 = jnp.bfloat16


def iota(shape, dim):
    return lax.broadcasted_iota(jnp.int32, shape, dim)


def fiota(shape, dim):
    return iota(shape, dim).astype(f32)


def dot_t(a, b):
    return lax.dot_general(a, b, (((1,), (1,)), ((), ())), preferred_element_type=f32)


def tdot(a, b):
    return lax.dot_general(a, b, (((0,), (0,)), ((), ())), preferred_element_type=f32)


def project_kernel(
    x_hbm, img_hbm, wq_hbm, wk_hbm, wv_hbm, gain_hbm, bq_hbm, bv_hbm, dest_hbm, invf_hbm, docs_hbm,
    kv_ref, share, aux, own,
    xs, wqs, wkvs, gains, bqs, bvs, dests, invfs, docs_ref, css, sems, small_sems,
):
    width = xs.shape[1]
    step = width // KCH
    copies = [
        pltpu.make_async_copy(x_hbm, xs.at[pl.ds(0, TOK)], sems.at[0]),
        pltpu.make_async_copy(img_hbm, xs.at[pl.ds(TOK, IMG)], sems.at[1]),
        pltpu.make_async_copy(wk_hbm, wkvs.at[pl.ds(0, 32)], sems.at[2]),
        pltpu.make_async_copy(wv_hbm, wkvs.at[pl.ds(32, 32)], sems.at[3]),
    ]
    for c in range(KCH):
        part = pl.ds(c * step, step)
        copies.append(pltpu.make_async_copy(wq_hbm.at[part], wqs.at[part], sems.at[4 + c]))
    small = [
        pltpu.make_async_copy(src, dst, small_sems.at[i])
        for i, (src, dst) in enumerate(
            ((docs_hbm, docs_ref), (dest_hbm, dests), (invf_hbm, invfs), (gain_hbm, gains), (bq_hbm, bqs), (bv_hbm, bvs))
        )
    ]
    for copy in small[:3] + copies[:2] + small[3:] + copies[2:]:
        copy.start()
    inverse = []
    for i, rows in enumerate((pl.ds(0, TOK), pl.ds(TOK, IMG))):
        copies[i].wait()
        squares = jnp.zeros((rows.size, HD), f32)
        for c in range(width // HD):
            wide = xs[rows, c * HD : (c + 1) * HD].astype(f32)
            squares = squares + wide * wide
        inverse.append(
            lax.rsqrt(jnp.sum(squares, axis=1, keepdims=True) * (1.0 / width) + norm_eps)
        )
    inverse = jnp.concatenate(inverse, axis=0)

    for copy in small[:3]:
        copy.wait()

    seq_place = lax.axis_index("seq")
    first = (seq_place * TOK).astype(f32)
    dest_row = dests[...].astype(f32)
    eye = iota((IMG, IMG), 0) == iota((IMG, IMG), 1)
    dest_col = jnp.sum(jnp.where(eye, dest_row, 0.0), axis=1, keepdims=True)
    hi_row = jnp.floor(dest_row * (1.0 / TOK))
    hi_col = jnp.floor(dest_col * (1.0 / TOK))
    lo_row = dest_row - TOK * hi_row
    lo_col = dest_col - TOK * hi_col

    index_col = jnp.concatenate([first + fiota((TOK, 1), 0), dest_col], axis=0)
    start_col = jnp.zeros((ROWS, 1), f32)
    begin = jnp.int32(0)
    for d in range(DOCS):
        begin_f = begin.astype(f32)
        start_col = jnp.where(index_col >= begin_f, begin_f, start_col)
        begin = begin + docs_ref[d]
    own[2 * TOK :, :] = jnp.broadcast_to(start_col[:TOK], (TOK, HD))
    angles = (index_col - start_col) * invfs[...]
    cosine = jnp.cos(angles)
    sine = jnp.sin(angles)
    sine = jnp.where(iota((ROWS, HD), 1) < HD // 2, -sine, sine)
    upper = (lax.axis_index("head") // 2) % 2 == 1
    for i, table in enumerate((cosine, sine)):
        css[i] = table
        low = i * KEYS
        aux[low : low + HALF_TOK, :] = jnp.where(upper, table[HALF_TOK:TOK], table[:HALF_TOK])
        aux[low + HALF_TOK : low + KEYS, :] = jnp.where(
            upper, table[TOK + HALF_IMG :], table[TOK : TOK + HALF_IMG]
        )

    for copy in small[3:] + copies[2:4]:
        copy.wait()
    queries = jnp.broadcast_to(bqs[...].astype(f32).reshape(1, 2 * HD), (ROWS, 2 * HD))
    kv = jnp.zeros((ROWS, 64), f32)
    for c in range(KCH):
        if c % 2 == 0:
            copies[4 + c].wait()
            copies[5 + c].wait()
        part = pl.ds(c * step, step)
        gain = gains[part].astype(f32).reshape(1, step)
        normed = (xs[:, part].astype(f32) * inverse * gain).astype(bf16)
        kv = kv + dot_t(normed, wkvs[:, part])
        queries = queries + jnp.dot(normed, wqs[part, :], preferred_element_type=f32)

    earlier = iota((IMG, IMG), 0) < iota((IMG, IMG), 1)
    later = iota((IMG, IMG), 0) > iota((IMG, IMG), 1)
    same = hi_col == hi_row
    rank_row = jnp.sum(jnp.where(same & earlier, 1.0, 0.0), axis=0, keepdims=True)
    rank_col = jnp.sum(jnp.where(same & later, 1.0, 0.0), axis=1, keepdims=True)
    count = N_SEQ * TAIL
    line = iota((count, IMG), 0)
    here = hi_row == (line // TAIL).astype(f32)
    slot = (line % TAIL).astype(f32)
    offsets = jnp.where(here & (slot == 14.0), lo_row + 1.0, 0.0).astype(bf16)
    lane = iota((IMG, HD), 1)
    ranked = jnp.where((rank_col == lane.astype(f32)) & (lane < CAP), 1.0, 0.0).astype(bf16)
    tail = jnp.dot(offsets, ranked, preferred_element_type=f32)
    skip = jnp.where(upper, HALF_IMG, 0)
    spread = (lane % 32 + skip == iota((IMG, HD), 0)) & (lane % 32 < HALF_IMG)
    unused = (iota((1, HD), 1) % 32) >= HALF_IMG
    hi_two = jnp.where(unused, 99.0, jnp.sum(jnp.where(spread, hi_col, 0.0), axis=0, keepdims=True))
    lo_two = jnp.sum(jnp.where(spread, lo_col, 0.0), axis=0, keepdims=True)
    wide_slot = iota((count, HD), 0) % TAIL
    tail = tail + jnp.where(wide_slot == 12, hi_two, jnp.where(wide_slot == 13, lo_two, 0.0))

    kv = jnp.concatenate([kv, jnp.zeros((ROWS, 64), f32)], axis=1)
    eye8 = iota((8, 8), 0) == iota((8, 8), 1)
    for j in range(2):
        kv_t = jnp.transpose(
            jnp.concatenate(
                [
                    kv[HALF_TOK * j : HALF_TOK * (j + 1)],
                    kv[TOK + HALF_IMG * j : TOK + HALF_IMG * (j + 1)],
                    jnp.zeros((HD - KEYS, HD), f32),
                ],
                axis=0,
            )
        )
        for g in range(4):
            bias_row = bvs[g : g + 1, :].astype(f32)
            bias = jnp.sum(jnp.where(eye8, bias_row, 0.0), axis=1, keepdims=True)
            kv_ref[4 * g + 2 * j] = kv_t[8 * g : 8 * g + 8].astype(bf16)
            kv_ref[4 * g + 2 * j + 1] = (kv_t[32 + 8 * g : 40 + 8 * g] + bias).astype(bf16)

    cosine = css[0]
    sine = css[1]
    for e in range(2):
        v = queries[:, e * HD : (e + 1) * HD]
        v = (v * cosine + pltpu.roll(v, HD // 2, 1) * sine).astype(bf16)
        share[e * TOK : (e + 1) * TOK, :] = v[:TOK]
        own[e * TOK : (e + 1) * TOK, :] = v[:TOK].astype(f32)
        pick = here & (rank_row == slot - CAP * e) & (slot >= CAP * e) & (slot < CAP * e + CAP)
        tail = tail + jnp.dot(
            jnp.where(pick, 1.0, 0.0).astype(bf16), v[TOK:], preferred_element_type=f32
        )
    share[2 * TOK :, :] = tail.astype(bf16)
    aux[2 * KEYS :, :] = tail


def panel_kernel(kv_ref, aux_ref, share_ref, pay_ref):
    is_key = lax.axis_index("head") % 2 == 0
    panel = jnp.transpose(kv_ref[...].astype(f32).reshape(HD, HD))[:KEYS]
    cosine = jnp.where(is_key, aux_ref[0:KEYS, :], 1.0)
    sine = jnp.where(is_key, aux_ref[KEYS : 2 * KEYS, :], 0.0)
    panel = (panel * cosine + pltpu.roll(panel, HD // 2, 1) * sine).astype(bf16)
    for p in range(N_SEQ):
        low = 2 * KEYS + TAIL * p
        pay_ref[p, 0:KEYS, :] = panel
        pay_ref[p, KEYS : KEYS + TAIL, :] = aux_ref[low : low + TAIL, :].astype(bf16)
        low = 2 * TOK + TAIL * p
        pay_ref[p, KEYS + TAIL : PAY, :] = share_ref[low : low + TAIL, :]


def place_kernel(own_ref, share_ref, mine_ref, mask_ref, merged_ref, where_ref, start_ref):
    start_ref[...] = own_ref[2 * TOK :, :]
    tails = mine_ref[:, KEYS:PAY, :].astype(f32)
    slots = tails[:, 14, :]
    count = N_SEQ * TAIL
    owner = iota((count, N_SEQ), 0) // TAIL == iota((count, N_SEQ), 1)
    spread = jnp.dot(
        jnp.where(owner, 1.0, 0.0).astype(bf16), slots.astype(bf16), preferred_element_type=f32
    )
    line = iota((count, HD), 0) % TAIL
    lane = iota((count, HD), 1)
    flats = [tails[:, c * TAIL : (c + 1) * TAIL, :].reshape(count, HD).astype(bf16) for c in range(2)]
    for e in range(2):
        slot = line - CAP * e
        used = (slot >= 0) & (slot < CAP)
        offset = jnp.sum(jnp.where(used & (lane == slot), spread, 0.0), axis=1, keepdims=True)
        place = jnp.where(offset == lane.astype(f32) + 1.0, 1.0, 0.0).astype(bf16)
        taken = tdot(place, jnp.ones((count, HD), bf16)) > 0.5
        span = slice(e * TOK, (e + 1) * TOK)
        merged_ref[span, :] = jnp.where(taken, tdot(place, flats[0]), own_ref[span, :]).astype(bf16)
        moved = jnp.where(taken, tdot(place, flats[1]), share_ref[span, :].astype(f32))
        merged_ref[(2 + e) * TOK : (3 + e) * TOK, :] = moved.astype(bf16)

    lane = iota((1, HD), 1)

    def four(rows, m):
        row = rows[4 * m + 3 : 4 * m + 4]
        for i in (2, 1, 0):
            row = jnp.where(lane < 32 * (i + 1), rows[4 * m + i : 4 * m + i + 1], row)
        return row

    covered = jnp.zeros((N_SEQ, HD), f32)
    for c in range(2):
        hi_all = tails[:, c * TAIL + 12, :]
        lo_all = tails[:, c * TAIL + 13, :]
        for m in range(N_SEQ // 4):
            hi = four(hi_all, m)
            lo = four(lo_all, m)
            hi_hot = jnp.where(hi == fiota((N_SEQ, HD), 0), 1.0, 0.0).astype(bf16)
            lo_hot = jnp.where(lo == fiota((HD, HD), 0), 1.0, 0.0).astype(bf16)
            covered = covered + dot_t(hi_hot, lo_hot)
            if c == 0:
                seen = jnp.zeros((1, HD), f32)
                for b in range(N_SEQ):
                    seen = jnp.where(hi == float(b), mask_ref[0, b].astype(f32), seen)
                at = N_SEQ // 2 + m
                where_ref[at : at + 1, :] = jnp.where(seen > 0.5, hi * float(TOK) + lo, BIG)
    upper = (lax.axis_index("head") // 2) % 2 == 1
    turned = pltpu.roll(covered, HALF_TOK, 1)
    near = jnp.where(upper, turned, covered)
    far = jnp.where(upper, covered, turned)
    base = (lane % HALF_TOK).astype(f32) + jnp.where(upper, float(HALF_TOK), 0.0)
    for m in range(N_SEQ // 2):
        left = lane < HALF_TOK
        taken = jnp.where(left, near[2 * m : 2 * m + 1], far[2 * m + 1 : 2 * m + 2])
        seen = jnp.where(left, mask_ref[0, 2 * m], mask_ref[0, 2 * m + 1])
        position = base + jnp.where(left, float(TOK * 2 * m), float(TOK * (2 * m + 1)))
        where_ref[m : m + 1, :] = jnp.where((taken < 0.5) & (seen == 1), position, BIG)


def attend_kernel(far, q_ref, where_ref, start_ref, mine_ref, other_ref, *rest):
    scores = rest[-1]
    count = 2 * TOK
    is_key = lax.axis_index("head") % 2 == 0
    first = (lax.axis_index("seq") * TOK).astype(f32)
    slope = math.log2(math.e) / math.sqrt(HD)

    low = jnp.maximum(lax.axis_index("seq") - REACH, 0) // 2
    low = jnp.minimum(low, PAIRS - WINDOW)

    def tile_of(ref, t):
        if t < WINDOW:
            return ref[pl.ds(2 * (low + t), 2), 0:HALF_TOK, :].reshape(HD, HD)
        m = t - WINDOW
        return ref[4 * m : 4 * m + 4, HALF_TOK : HALF_TOK + 32, :].reshape(HD, HD)

    def where_of(t):
        if t < WINDOW:
            return where_ref[pl.ds(low + t, 1), :]
        return where_ref[PAIRS + t - WINDOW : PAIRS + t - WINDOW + 1, :]

    steps = WINDOW + N_SEQ // 4

    def attend(keys, values):
        queries = q_ref[count:, :] if far else q_ref[:count, :]
        position = first + fiota((TOK, HD), 0)
        start = start_ref[...]
        top = jnp.full((count, HD), NEG, f32)
        for t in range(steps):
            where = where_of(t)
            allowed = (where <= position) & (where >= start)
            allowed = jnp.concatenate([allowed] * 2, axis=0)
            score = jnp.where(allowed, dot_t(queries, tile_of(keys, t)), NEG)
            scores[t] = score
            top = jnp.maximum(top, score)
        top = jnp.maximum(jnp.max(top, axis=1, keepdims=True), LOW)
        total = jnp.zeros((count, HD), f32)
        mix = jnp.zeros((count, HD), f32)
        for t in range(steps):
            weight = jnp.exp2((scores[t] - top) * slope)
            total = total + weight
            mix = mix + jnp.dot(weight.astype(bf16), tile_of(values, t), preferred_element_type=f32)
        total = jnp.sum(total, axis=1, keepdims=True)
        if not far:
            keep_ref = rest[0]
            keep_ref[0] = mix
            keep_ref[1] = jnp.broadcast_to(top, (count, HD))
            keep_ref[2] = jnp.broadcast_to(total, (count, HD))
            return
        send_ref = rest[0]
        send_ref[0:count, :] = (mix / jnp.maximum(total, 1.0e-30)).astype(bf16)
        rows = []
        for column in (top, total):
            for e in range(2):
                part = jnp.broadcast_to(column[e * TOK : (e + 1) * TOK], (TOK, HD))
                left = jnp.transpose(part)[0:1]
                for _ in range(3):
                    piece = left.astype(bf16).astype(f32)
                    rows.append(piece)
                    left = left - piece
        rows.append(jnp.zeros((4, HD), f32))
        send_ref[count:, :] = jnp.concatenate(rows, axis=0).astype(bf16)

    @pl.when(is_key)
    def _():
        attend(mine_ref, other_ref)

    @pl.when(jnp.logical_not(is_key))
    def _():
        attend(other_ref, mine_ref)


def combine_kernel(keep_ref, come_ref, out_hbm, halves, sems):
    slope = math.log2(math.e) / math.sqrt(HD)
    pieces = come_ref[2 * TOK :, :].astype(f32)

    def column(i):
        row = pieces[3 * i : 3 * i + 1] + pieces[3 * i + 1 : 3 * i + 2] + pieces[3 * i + 2 : 3 * i + 3]
        return jnp.transpose(jnp.broadcast_to(row, (TOK, HD)))

    copies = []
    for e in range(2):
        span = slice(e * TOK, (e + 1) * TOK)
        top_near = keep_ref[1, span, :]
        top_far = column(e)
        top = jnp.maximum(top_near, top_far)
        near = jnp.exp2((top_near - top) * slope)
        far = jnp.exp2((top_far - top) * slope) * column(2 + e)
        mix = keep_ref[0, span, :] * near + come_ref[span, :].astype(f32) * far
        halves[e] = (mix / (keep_ref[2, span, :] * near + far)).astype(bf16)
        copies.append(
            pltpu.make_async_copy(
                halves.at[e], out_hbm.at[:, pl.ds(e * HD, HD)], sems.at[e]
            )
        )
        copies[e].start()
    for copy in copies:
        copy.wait()


def vmem():
    return pl.BlockSpec(memory_space=pltpu.VMEM)


def small_params():
    return pltpu.CompilerParams(vmem_limit_bytes=SMALL)


def project_call(width):
    hbm = pl.BlockSpec(memory_space=pltpu.HBM)
    outputs = [
        ((N_HEAD, 8, HD), bf16),
        ((2 * TOK + N_SEQ * TAIL, HD), bf16),
        ((2 * KEYS + N_SEQ * TAIL, HD), f32),
        ((3 * TOK, HD), f32),
    ]
    call = pl.pallas_call(
        project_kernel,
        name="project",
        out_shape=tuple(jax.ShapeDtypeStruct(shape, dtype) for shape, dtype in outputs),
        in_specs=[hbm] * 11,
        out_specs=(vmem(),) * 4,
        scratch_shapes=[
            pltpu.VMEM((ROWS, width), bf16),
            pltpu.VMEM((width, 2 * HD), bf16),
            pltpu.VMEM((64, width), bf16),
            pltpu.VMEM((width,), bf16),
            pltpu.VMEM((2 * HD,), bf16),
            pltpu.VMEM((4, 8), bf16),
            pltpu.VMEM((1, IMG), jnp.int32),
            pltpu.VMEM((1, HD), f32),
            pltpu.SMEM((DOCS,), jnp.int32),
            pltpu.VMEM((2, ROWS, HD), f32),
            pltpu.SemaphoreType.DMA((4 + KCH,)),
            pltpu.SemaphoreType.DMA((6,)),
        ],
        compiler_params=pltpu.CompilerParams(vmem_limit_bytes=20 << 20),
    )
    return lambda *arrays: call(
        *(pltpu.with_memory_space_constraint(array, pltpu.HBM) for array in arrays)
    )


def attend_call(far):
    out = ((2 * TOK + 16, HD), bf16) if far else ((3, 2 * TOK, HD), f32)
    return pl.pallas_call(
        functools.partial(attend_kernel, far),
        name="attend_far" if far else "attend_near",
        out_shape=jax.ShapeDtypeStruct(*out),
        in_specs=[vmem()] * 5,
        out_specs=vmem(),
        scratch_shapes=[pltpu.VMEM((WINDOW + N_SEQ // 4, 2 * TOK, HD), f32)],
        compiler_params=small_params(),
        cost_estimate=pl.CostEstimate(flops=1 << 30, bytes_accessed=1 << 21, transcendentals=1 << 19),
    )


def panel_call():
    return pl.pallas_call(
        panel_kernel,
        name="panel",
        out_shape=jax.ShapeDtypeStruct((N_SEQ, PAY, HD), bf16),
        in_specs=[vmem()] * 3,
        out_specs=vmem(),
        compiler_params=small_params(),
    )


def body(
    embedded,
    norm_gain,
    query_weight,
    query_bias,
    key_weight,
    value_weight,
    value_bias,
    image_rows,
    image_dest,
    doc_lengths,
    block_mask,
):
    width = embedded.shape[1]
    half = np.arange(HD) % (HD // 2)
    inverse = jnp.asarray((rope_base ** (-2.0 * half / HD)).astype(np.float32)[None, :])
    smem = pl.BlockSpec(memory_space=pltpu.SMEM)
    key_t = jnp.transpose(key_weight, (1, 2, 0)).reshape(32, width)
    value_t = jnp.transpose(value_weight, (1, 2, 0)).reshape(32, width)
    kv_send, share, aux, own = project_call(width)(
        embedded, image_rows, query_weight, key_t, value_t, norm_gain, query_bias,
        value_bias, image_dest[None, :], inverse, doc_lengths,
    )
    chip_swap = [(i, i ^ 2) for i in range(N_HEAD)]
    core_swap = [(i, i ^ 1) for i in range(N_HEAD)]
    shared = lax.ppermute(share, "head", chip_swap)
    kv_mine = lax.all_to_all(kv_send, "head", 0, 0)
    payload = panel_call()(kv_mine, aux, shared)
    mine = lax.all_to_all(payload, "seq", 0, 0)
    other = lax.ppermute(mine, "head", core_swap)
    merged, where, start = pl.pallas_call(
        place_kernel,
        name="place",
        out_shape=(
            jax.ShapeDtypeStruct((4 * TOK, HD), bf16),
            jax.ShapeDtypeStruct((TILES, HD), f32),
            jax.ShapeDtypeStruct((TOK, HD), f32),
        ),
        in_specs=[vmem()] * 3 + [smem],
        out_specs=(vmem(),) * 3,
        compiler_params=small_params(),
        cost_estimate=pl.CostEstimate(flops=1 << 28, bytes_accessed=1 << 20, transcendentals=0),
    )(own, shared, mine, block_mask)
    send = attend_call(True)(merged, where, start, mine, other)
    come = lax.ppermute(send, "head", chip_swap)
    keep = attend_call(False)(merged, where, start, mine, other)
    return pl.pallas_call(
        combine_kernel,
        name="combine",
        out_shape=jax.ShapeDtypeStruct((TOK, 2 * HD), bf16),
        in_specs=[vmem()] * 2,
        out_specs=pl.BlockSpec(memory_space=pltpu.HBM),
        scratch_shapes=[pltpu.VMEM((2, TOK, HD), bf16), pltpu.SemaphoreType.DMA((2,))],
        compiler_params=small_params(),
    )(keep, come)


def solution(mesh):
    in_specs = (
        P("seq", None),
        P(),
        P(None, "head"),
        P("head"),
        P(None, None, "head"),
        P(None, None, "head"),
        P(None, "head"),
        P("seq", None),
        P("seq"),
        P(),
        P("seq", None),
    )
    out_specs = P("seq", "head")
    return jax.shard_map(body, mesh=mesh, in_specs=in_specs, out_specs=out_specs, check_vma=False)
```

```python
import functools
import math

import jax
import jax.numpy as jnp
import numpy as np
from jax import lax
from jax.experimental import pallas as pl
from jax.experimental.pallas import tpu as pltpu
from jax.sharding import PartitionSpec as P

HD = 128
GROUP = 8
BLK = 128
CAP = 6
TOK = 128
IMG = 48
N_SEQ = 16
N_HEAD = 16
ROWS = TOK + IMG
HALF_TOK = TOK // 2
HALF_IMG = IMG // 2
KEYS = HALF_TOK + HALF_IMG
TAIL = 16
PAY = KEYS + 2 * TAIL
PAIRS = N_SEQ // 2
TILES = PAIRS + N_SEQ // 4
MOST_DOC = 1152
REACH = MOST_DOC // TOK
WINDOW = REACH // 2 + 2
DOCS = 32
KCH = 4
LIMIT = 60 << 20
SMALL = 12 << 20

rope_base = 1000000.0
norm_eps = 1e-06
BIG = 1.0e6
NEG = -1.0e30
LOW = -1.0e29

f32 = jnp.float32
bf16 = jnp.bfloat16


def iota(shape, dim):
    return lax.broadcasted_iota(jnp.int32, shape, dim)


def fiota(shape, dim):
    return iota(shape, dim).astype(f32)


def dot_t(a, b):
    return lax.dot_general(a, b, (((1,), (1,)), ((), ())), preferred_element_type=f32)


def tdot(a, b):
    return lax.dot_general(a, b, (((0,), (0,)), ((), ())), preferred_element_type=f32)


def project_kernel(
    x_hbm, img_hbm, wq_hbm, wk_hbm, wv_hbm, gain_hbm, bq_hbm, bv_hbm, dest_hbm, invf_hbm, docs_hbm,
    kv_ref, share, aux, own,
    xs, wqs, wkvs, gains, bqs, bvs, dests, invfs, docs_ref, css, sems, small_sems,
):
    width = xs.shape[1]
    step = width // KCH
    copies = [
        pltpu.make_async_copy(x_hbm, xs.at[pl.ds(0, TOK)], sems.at[0]),
        pltpu.make_async_copy(img_hbm, xs.at[pl.ds(TOK, IMG)], sems.at[1]),
        pltpu.make_async_copy(wk_hbm, wkvs.at[pl.ds(0, 32)], sems.at[2]),
        pltpu.make_async_copy(wv_hbm, wkvs.at[pl.ds(32, 32)], sems.at[3]),
    ]
    for c in range(KCH):
        part = pl.ds(c * step, step)
        copies.append(pltpu.make_async_copy(wq_hbm.at[part], wqs.at[part], sems.at[4 + c]))
    small = [
        pltpu.make_async_copy(src, dst, small_sems.at[i])
        for i, (src, dst) in enumerate(
            ((docs_hbm, docs_ref), (dest_hbm, dests), (invf_hbm, invfs), (gain_hbm, gains), (bq_hbm, bqs), (bv_hbm, bvs))
        )
    ]
    for copy in small[:3] + copies[:2] + small[3:] + copies[2:]:
        copy.start()
    inverse = []
    for i, rows in enumerate((pl.ds(0, TOK), pl.ds(TOK, IMG))):
        copies[i].wait()
        squares = jnp.zeros((rows.size, HD), f32)
        for c in range(width // HD):
            wide = xs[rows, c * HD : (c + 1) * HD].astype(f32)
            squares = squares + wide * wide
        inverse.append(
            lax.rsqrt(jnp.sum(squares, axis=1, keepdims=True) * (1.0 / width) + norm_eps)
        )
    inverse = jnp.concatenate(inverse, axis=0)

    for copy in small[:3]:
        copy.wait()

    seq_place = lax.axis_index("seq")
    first = (seq_place * TOK).astype(f32)
    dest_row = dests[...].astype(f32)
    eye = iota((IMG, IMG), 0) == iota((IMG, IMG), 1)
    dest_col = jnp.sum(jnp.where(eye, dest_row, 0.0), axis=1, keepdims=True)
    hi_row = jnp.floor(dest_row * (1.0 / TOK))
    hi_col = jnp.floor(dest_col * (1.0 / TOK))
    lo_row = dest_row - TOK * hi_row
    lo_col = dest_col - TOK * hi_col

    index_col = jnp.concatenate([first + fiota((TOK, 1), 0), dest_col], axis=0)
    start_col = jnp.zeros((ROWS, 1), f32)
    begin = jnp.int32(0)
    for d in range(DOCS):
        begin_f = begin.astype(f32)
        start_col = jnp.where(index_col >= begin_f, begin_f, start_col)
        begin = begin + docs_ref[d]
    own[2 * TOK :, :] = jnp.broadcast_to(start_col[:TOK], (TOK, HD))
    angles = (index_col - start_col) * invfs[...]
    cosine = jnp.cos(angles)
    sine = jnp.sin(angles)
    sine = jnp.where(iota((ROWS, HD), 1) < HD // 2, -sine, sine)
    upper = (lax.axis_index("head") // 2) % 2 == 1
    for i, table in enumerate((cosine, sine)):
        css[i] = table
        low = i * KEYS
        aux[low : low + HALF_TOK, :] = jnp.where(upper, table[HALF_TOK:TOK], table[:HALF_TOK])
        aux[low + HALF_TOK : low + KEYS, :] = jnp.where(
            upper, table[TOK + HALF_IMG :], table[TOK : TOK + HALF_IMG]
        )

    for copy in small[3:] + copies[2:4]:
        copy.wait()
    queries = jnp.broadcast_to(bqs[...].astype(f32).reshape(1, 2 * HD), (ROWS, 2 * HD))
    kv = jnp.zeros((ROWS, 64), f32)
    for c in range(KCH):
        if c % 2 == 0:
            copies[4 + c].wait()
            copies[5 + c].wait()
        part = pl.ds(c * step, step)
        gain = gains[part].astype(f32).reshape(1, step)
        normed = (xs[:, part].astype(f32) * inverse * gain).astype(bf16)
        kv = kv + dot_t(normed, wkvs[:, part])
        queries = queries + jnp.dot(normed, wqs[part, :], preferred_element_type=f32)

    earlier = iota((IMG, IMG), 0) < iota((IMG, IMG), 1)
    later = iota((IMG, IMG), 0) > iota((IMG, IMG), 1)
    same = hi_col == hi_row
    rank_row = jnp.sum(jnp.where(same & earlier, 1.0, 0.0), axis=0, keepdims=True)
    rank_col = jnp.sum(jnp.where(same & later, 1.0, 0.0), axis=1, keepdims=True)
    count = N_SEQ * TAIL
    line = iota((count, IMG), 0)
    here = hi_row == (line // TAIL).astype(f32)
    slot = (line % TAIL).astype(f32)
    offsets = jnp.where(here & (slot == 14.0), lo_row + 1.0, 0.0).astype(bf16)
    lane = iota((IMG, HD), 1)
    ranked = jnp.where((rank_col == lane.astype(f32)) & (lane < CAP), 1.0, 0.0).astype(bf16)
    tail = jnp.dot(offsets, ranked, preferred_element_type=f32)
    skip = jnp.where(upper, HALF_IMG, 0)
    spread = (lane % 32 + skip == iota((IMG, HD), 0)) & (lane % 32 < HALF_IMG)
    unused = (iota((1, HD), 1) % 32) >= HALF_IMG
    hi_two = jnp.where(unused, 99.0, jnp.sum(jnp.where(spread, hi_col, 0.0), axis=0, keepdims=True))
    lo_two = jnp.sum(jnp.where(spread, lo_col, 0.0), axis=0, keepdims=True)
    wide_slot = iota((count, HD), 0) % TAIL
    tail = tail + jnp.where(wide_slot == 12, hi_two, jnp.where(wide_slot == 13, lo_two, 0.0))

    kv = jnp.concatenate([kv, jnp.zeros((ROWS, 64), f32)], axis=1)
    eye8 = iota((8, 8), 0) == iota((8, 8), 1)
    for j in range(2):
        kv_t = jnp.transpose(
            jnp.concatenate(
                [
                    kv[HALF_TOK * j : HALF_TOK * (j + 1)],
                    kv[TOK + HALF_IMG * j : TOK + HALF_IMG * (j + 1)],
                    jnp.zeros((HD - KEYS, HD), f32),
                ],
                axis=0,
            )
        )
        for g in range(4):
            bias_row = bvs[g : g + 1, :].astype(f32)
            bias = jnp.sum(jnp.where(eye8, bias_row, 0.0), axis=1, keepdims=True)
            kv_ref[4 * g + 2 * j] = kv_t[8 * g : 8 * g + 8].astype(bf16)
            kv_ref[4 * g + 2 * j + 1] = (kv_t[32 + 8 * g : 40 + 8 * g] + bias).astype(bf16)

    cosine = css[0]
    sine = css[1]
    for e in range(2):
        v = queries[:, e * HD : (e + 1) * HD]
        v = (v * cosine + pltpu.roll(v, HD // 2, 1) * sine).astype(bf16)
        share[e * TOK : (e + 1) * TOK, :] = v[:TOK]
        own[e * TOK : (e + 1) * TOK, :] = v[:TOK].astype(f32)
        pick = here & (rank_row == slot - CAP * e) & (slot >= CAP * e) & (slot < CAP * e + CAP)
        tail = tail + jnp.dot(
            jnp.where(pick, 1.0, 0.0).astype(bf16), v[TOK:], preferred_element_type=f32
        )
    share[2 * TOK :, :] = tail.astype(bf16)
    aux[2 * KEYS :, :] = tail


def panel_kernel(kv_ref, aux_ref, share_ref, pay_ref):
    is_key = lax.axis_index("head") % 2 == 0
    panel = jnp.transpose(kv_ref[...].astype(f32).reshape(HD, HD))[:KEYS]
    cosine = jnp.where(is_key, aux_ref[0:KEYS, :], 1.0)
    sine = jnp.where(is_key, aux_ref[KEYS : 2 * KEYS, :], 0.0)
    panel = (panel * cosine + pltpu.roll(panel, HD // 2, 1) * sine).astype(bf16)
    for p in range(N_SEQ):
        low = 2 * KEYS + TAIL * p
        pay_ref[p, 0:KEYS, :] = panel
        pay_ref[p, KEYS : KEYS + TAIL, :] = aux_ref[low : low + TAIL, :].astype(bf16)
        low = 2 * TOK + TAIL * p
        pay_ref[p, KEYS + TAIL : PAY, :] = share_ref[low : low + TAIL, :]


def place_kernel(own_ref, share_ref, mine_ref, mask_ref, merged_ref, where_ref, start_ref):
    start_ref[...] = own_ref[2 * TOK :, :]
    tails = mine_ref[:, KEYS:PAY, :].astype(f32)
    slots = tails[:, 14, :]
    count = N_SEQ * TAIL
    owner = iota((count, N_SEQ), 0) // TAIL == iota((count, N_SEQ), 1)
    spread = jnp.dot(
        jnp.where(owner, 1.0, 0.0).astype(bf16), slots.astype(bf16), preferred_element_type=f32
    )
    line = iota((count, HD), 0) % TAIL
    lane = iota((count, HD), 1)
    flats = [tails[:, c * TAIL : (c + 1) * TAIL, :].reshape(count, HD).astype(bf16) for c in range(2)]
    for e in range(2):
        slot = line - CAP * e
        used = (slot >= 0) & (slot < CAP)
        offset = jnp.sum(jnp.where(used & (lane == slot), spread, 0.0), axis=1, keepdims=True)
        place = jnp.where(offset == lane.astype(f32) + 1.0, 1.0, 0.0).astype(bf16)
        taken = tdot(place, jnp.ones((count, HD), bf16)) > 0.5
        span = slice(e * TOK, (e + 1) * TOK)
        merged_ref[span, :] = jnp.where(taken, tdot(place, flats[0]), own_ref[span, :]).astype(bf16)
        moved = jnp.where(taken, tdot(place, flats[1]), share_ref[span, :].astype(f32))
        merged_ref[(2 + e) * TOK : (3 + e) * TOK, :] = moved.astype(bf16)

    lane = iota((1, HD), 1)

    def four(rows, m):
        row = rows[4 * m + 3 : 4 * m + 4]
        for i in (2, 1, 0):
            row = jnp.where(lane < 32 * (i + 1), rows[4 * m + i : 4 * m + i + 1], row)
        return row

    covered = jnp.zeros((N_SEQ, HD), f32)
    for c in range(2):
        hi_all = tails[:, c * TAIL + 12, :]
        lo_all = tails[:, c * TAIL + 13, :]
        for m in range(N_SEQ // 4):
            hi = four(hi_all, m)
            lo = four(lo_all, m)
            hi_hot = jnp.where(hi == fiota((N_SEQ, HD), 0), 1.0, 0.0).astype(bf16)
            lo_hot = jnp.where(lo == fiota((HD, HD), 0), 1.0, 0.0).astype(bf16)
            covered = covered + dot_t(hi_hot, lo_hot)
            if c == 0:
                seen = jnp.zeros((1, HD), f32)
                for b in range(N_SEQ):
                    seen = jnp.where(hi == float(b), mask_ref[0, b].astype(f32), seen)
                at = N_SEQ // 2 + m
                where_ref[at : at + 1, :] = jnp.where(seen > 0.5, hi * float(TOK) + lo, BIG)
    upper = (lax.axis_index("head") // 2) % 2 == 1
    turned = pltpu.roll(covered, HALF_TOK, 1)
    near = jnp.where(upper, turned, covered)
    far = jnp.where(upper, covered, turned)
    base = (lane % HALF_TOK).astype(f32) + jnp.where(upper, float(HALF_TOK), 0.0)
    for m in range(N_SEQ // 2):
        left = lane < HALF_TOK
        taken = jnp.where(left, near[2 * m : 2 * m + 1], far[2 * m + 1 : 2 * m + 2])
        seen = jnp.where(left, mask_ref[0, 2 * m], mask_ref[0, 2 * m + 1])
        position = base + jnp.where(left, float(TOK * 2 * m), float(TOK * (2 * m + 1)))
        where_ref[m : m + 1, :] = jnp.where((taken < 0.5) & (seen == 1), position, BIG)


def attend_kernel(far, q_ref, where_ref, start_ref, mine_ref, other_ref, *rest):
    scores = rest[-1]
    count = 2 * TOK
    is_key = lax.axis_index("head") % 2 == 0
    first = (lax.axis_index("seq") * TOK).astype(f32)
    slope = math.log2(math.e) / math.sqrt(HD)

    low = jnp.maximum(lax.axis_index("seq") - REACH, 0) // 2
    low = jnp.minimum(low, PAIRS - WINDOW)

    def tile_of(ref, t):
        if t < WINDOW:
            return ref[pl.ds(2 * (low + t), 2), 0:HALF_TOK, :].reshape(HD, HD)
        m = t - WINDOW
        return ref[4 * m : 4 * m + 4, HALF_TOK : HALF_TOK + 32, :].reshape(HD, HD)

    def where_of(t):
        if t < WINDOW:
            return where_ref[pl.ds(low + t, 1), :]
        return where_ref[PAIRS + t - WINDOW : PAIRS + t - WINDOW + 1, :]

    steps = WINDOW + N_SEQ // 4

    def attend(keys, values):
        queries = q_ref[count:, :] if far else q_ref[:count, :]
        position = first + fiota((TOK, HD), 0)
        start = start_ref[...]
        top = jnp.full((count, HD), NEG, f32)
        for t in range(steps):
            where = where_of(t)
            allowed = (where <= position) & (where >= start)
            allowed = jnp.concatenate([allowed] * 2, axis=0)
            score = jnp.where(allowed, dot_t(queries, tile_of(keys, t)), NEG)
            scores[t] = score
            top = jnp.maximum(top, score)
        top = jnp.maximum(jnp.max(top, axis=1, keepdims=True), LOW)
        total = jnp.zeros((count, HD), f32)
        mix = jnp.zeros((count, HD), f32)
        for t in range(steps):
            weight = jnp.exp2((scores[t] - top) * slope)
            total = total + weight
            mix = mix + jnp.dot(weight.astype(bf16), tile_of(values, t), preferred_element_type=f32)
        total = jnp.sum(total, axis=1, keepdims=True)
        if not far:
            keep_ref = rest[0]
            keep_ref[0] = mix
            keep_ref[1] = jnp.broadcast_to(top, (count, HD))
            keep_ref[2] = jnp.broadcast_to(total, (count, HD))
            return
        send_ref = rest[0]
        send_ref[0:count, :] = (mix * (1.0 / jnp.maximum(total, 1.0e-30))).astype(bf16)
        rows = []
        for column in (top, total):
            for e in range(2):
                part = jnp.broadcast_to(column[e * TOK : (e + 1) * TOK], (TOK, HD))
                left = jnp.transpose(part)[0:1]
                for _ in range(3):
                    piece = left.astype(bf16).astype(f32)
                    rows.append(piece)
                    left = left - piece
        rows.append(jnp.zeros((4, HD), f32))
        send_ref[count:, :] = jnp.concatenate(rows, axis=0).astype(bf16)

    @pl.when(is_key)
    def _():
        attend(mine_ref, other_ref)

    @pl.when(jnp.logical_not(is_key))
    def _():
        attend(other_ref, mine_ref)


def combine_kernel(keep_ref, come_ref, out_ref):
    slope = math.log2(math.e) / math.sqrt(HD)
    pieces = come_ref[2 * TOK :, :].astype(f32)

    def column(i):
        row = pieces[3 * i : 3 * i + 1] + pieces[3 * i + 1 : 3 * i + 2] + pieces[3 * i + 2 : 3 * i + 3]
        return jnp.transpose(jnp.broadcast_to(row, (TOK, HD)))

    for e in range(2):
        span = slice(e * TOK, (e + 1) * TOK)
        top_near = keep_ref[1, span, :]
        top_far = column(e)
        top = jnp.maximum(top_near, top_far)
        near = jnp.exp2((top_near - top) * slope)
        far = jnp.exp2((top_far - top) * slope) * column(2 + e)
        mix = keep_ref[0, span, :] * near + come_ref[span, :].astype(f32) * far
        out_ref[:, e * HD : (e + 1) * HD] = (mix / (keep_ref[2, span, :] * near + far)).astype(bf16)


def vmem():
    return pl.BlockSpec(memory_space=pltpu.VMEM)


def small_params():
    return pltpu.CompilerParams(vmem_limit_bytes=SMALL)


def project_call(width):
    hbm = pl.BlockSpec(memory_space=pltpu.HBM)
    outputs = [
        ((N_HEAD, 8, HD), bf16),
        ((2 * TOK + N_SEQ * TAIL, HD), bf16),
        ((2 * KEYS + N_SEQ * TAIL, HD), f32),
        ((3 * TOK, HD), f32),
    ]
    call = pl.pallas_call(
        project_kernel,
        name="project",
        out_shape=tuple(jax.ShapeDtypeStruct(shape, dtype) for shape, dtype in outputs),
        in_specs=[hbm] * 11,
        out_specs=(vmem(),) * 4,
        scratch_shapes=[
            pltpu.VMEM((ROWS, width), bf16),
            pltpu.VMEM((width, 2 * HD), bf16),
            pltpu.VMEM((64, width), bf16),
            pltpu.VMEM((width,), bf16),
            pltpu.VMEM((2 * HD,), bf16),
            pltpu.VMEM((4, 8), bf16),
            pltpu.VMEM((1, IMG), jnp.int32),
            pltpu.VMEM((1, HD), f32),
            pltpu.SMEM((DOCS,), jnp.int32),
            pltpu.VMEM((2, ROWS, HD), f32),
            pltpu.SemaphoreType.DMA((4 + KCH,)),
            pltpu.SemaphoreType.DMA((6,)),
        ],
        compiler_params=pltpu.CompilerParams(vmem_limit_bytes=20 << 20),
    )
    return lambda *arrays: call(
        *(pltpu.with_memory_space_constraint(array, pltpu.HBM) for array in arrays)
    )


def attend_call(far):
    out = ((2 * TOK + 16, HD), bf16) if far else ((3, 2 * TOK, HD), f32)
    return pl.pallas_call(
        functools.partial(attend_kernel, far),
        name="attend_far" if far else "attend_near",
        out_shape=jax.ShapeDtypeStruct(*out),
        in_specs=[vmem()] * 5,
        out_specs=vmem(),
        scratch_shapes=[pltpu.VMEM((WINDOW + N_SEQ // 4, 2 * TOK, HD), f32)],
        compiler_params=small_params(),
        cost_estimate=pl.CostEstimate(flops=1 << 30, bytes_accessed=1 << 21, transcendentals=1 << 19),
    )


def panel_call():
    return pl.pallas_call(
        panel_kernel,
        name="panel",
        out_shape=jax.ShapeDtypeStruct((N_SEQ, PAY, HD), bf16),
        in_specs=[vmem()] * 3,
        out_specs=vmem(),
        compiler_params=small_params(),
    )


def body(
    embedded,
    norm_gain,
    query_weight,
    query_bias,
    key_weight,
    value_weight,
    value_bias,
    image_rows,
    image_dest,
    doc_lengths,
    block_mask,
):
    width = embedded.shape[1]
    half = np.arange(HD) % (HD // 2)
    inverse = jnp.asarray((rope_base ** (-2.0 * half / HD)).astype(np.float32)[None, :])
    smem = pl.BlockSpec(memory_space=pltpu.SMEM)
    key_t = jnp.transpose(key_weight, (1, 2, 0)).reshape(32, width)
    value_t = jnp.transpose(value_weight, (1, 2, 0)).reshape(32, width)
    kv_send, share, aux, own = project_call(width)(
        embedded, image_rows, query_weight, key_t, value_t, norm_gain, query_bias,
        value_bias, image_dest[None, :], inverse, doc_lengths,
    )
    chip_swap = [(i, i ^ 2) for i in range(N_HEAD)]
    core_swap = [(i, i ^ 1) for i in range(N_HEAD)]
    shared = lax.ppermute(share, "head", chip_swap)
    kv_mine = lax.all_to_all(kv_send, "head", 0, 0)
    payload = panel_call()(kv_mine, aux, shared)
    mine = lax.all_to_all(payload, "seq", 0, 0)
    other = lax.ppermute(mine, "head", core_swap)
    merged, where, start = pl.pallas_call(
        place_kernel,
        name="place",
        out_shape=(
            jax.ShapeDtypeStruct((4 * TOK, HD), bf16),
            jax.ShapeDtypeStruct((TILES, HD), f32),
            jax.ShapeDtypeStruct((TOK, HD), f32),
        ),
        in_specs=[vmem()] * 3 + [smem],
        out_specs=(vmem(),) * 3,
        compiler_params=small_params(),
        cost_estimate=pl.CostEstimate(flops=1 << 28, bytes_accessed=1 << 20, transcendentals=0),
    )(own, shared, mine, block_mask)
    send = attend_call(True)(merged, where, start, mine, other)
    come = lax.ppermute(send, "head", chip_swap)
    keep = attend_call(False)(merged, where, start, mine, other)
    return pl.pallas_call(
        combine_kernel,
        name="combine",
        out_shape=jax.ShapeDtypeStruct((TOK, 2 * HD), bf16),
        in_specs=[vmem()] * 2,
        out_specs=vmem(),
        compiler_params=small_params(),
    )(keep, come)


def solution(mesh):
    in_specs = (
        P("seq", None),
        P(),
        P(None, "head"),
        P("head"),
        P(None, None, "head"),
        P(None, None, "head"),
        P(None, "head"),
        P("seq", None),
        P("seq"),
        P(),
        P("seq", None),
    )
    out_specs = P("seq", "head")
    return jax.shard_map(body, mesh=mesh, in_specs=in_specs, out_specs=out_specs, check_vma=False)
```
